256 devices in a mesh: band: 8 (over z), dev: 32 (over x, y, core).
Axes of the slice: x: 4, y: 4, z: 8, core: 2. Of those that a mesh axis runs over, the one named last changes fastest.
Arguments:
- anomaly: float32 [256, 1048576], P('dev', 'band'), may hold values from -6 to 6
- ocean_mask: int32 [1048576], P('band'), may hold values 0 or 1
- area_weight: float32 [1048576], P('band'), may hold values from 0.02 to 1
Outputs:
- factor: float32 [256, 256], replicated
- scores: float32 [256, 1048576], P(None, ('band', 'dev'))
The draws below stay inside these ranges and needn't reach their ends.
All inputs are finite; a program needn't handle non-finite values. No bound on the sum of `ocean_mask` on one device may be relied on, other than what follows from the above.
Results may differ from the reference program's by a relative error of at most 0.000075.
Values sent between devices are 32-bit elements; how exact they have to be, the bound alone decides.
A program may use at most 64 MiB of HBM per device.

```python
import math
import jax
import jax.numpy as jnp
from jax import lax

SNAPS = 256
CELLS = 1048576


def place_ends(array, rng, least, top_value):
    dims = array.shape
    index_at = [jax.random.randint(jax.random.fold_in(rng, axis), (), 0, dims[axis]) for axis in range(len(dims))]
    array = array.at[tuple(index_at)].set(least)
    longest = dims.index(max(dims))
    index_at[longest] = (index_at[longest] + 1) % dims[longest]
    return array.at[tuple(index_at)].set(top_value)


def steps_of(rng, dims, cuts, low, largest):
    factor_of, own = 1.0, jax.random.fold_in(rng, 6)
    for axis_at, blocks in cuts:
        steps = jnp.exp(jax.random.uniform(jax.random.fold_in(own, axis_at), (blocks,), jnp.float32, low / len(cuts), largest / len(cuts)))
        factor_of = factor_of * jnp.repeat(steps, dims[axis_at] // blocks).reshape([-1 if axis == axis_at else 1 for axis in range(len(dims))])
    return factor_of


def normal_values(own_key, extent, spread, limit, shards=(), kind=jnp.bfloat16):
    gain = steps_of(own_key, extent, shards, -0.22, 0.18) if shards else 1.0
    array = jax.random.normal(own_key, extent, jnp.float32) * spread * gain
    return jnp.minimum(jnp.maximum(array, -limit), limit).astype(kind)


def setup_inputs(seed: int = 0) -> dict:
    splits = jax.random.split(jax.random.key(seed), 4)
    anomaly = normal_values(splits[0], (SNAPS, CELLS), 1.0, 6.0, ((0, 32), (1, 8)), jnp.float32)
    ocean_mask = place_ends((jax.random.randint(splits[1], (CELLS,), 0, 3) < 2).astype(jnp.int32), jax.random.fold_in(splits[1], 1), 0, 1)
    area_weight = jnp.clip(jnp.exp(math.log(1.0) - 3.912023 * jax.random.uniform(splits[2], (CELLS,), jnp.float32) ** steps_of(splits[2], (CELLS,), ((0, 8),), -0.2, 0.2)), 0.02, 1.0)
    return {"anomaly": anomaly, "ocean_mask": ocean_mask, "area_weight": area_weight}


def reference(anomaly, ocean_mask, area_weight):
    weights = area_weight * ocean_mask.astype(jnp.float32)
    scaled = anomaly * jnp.sqrt(weights)[None, :]
    total = jnp.sum(weights)
    gram = jnp.dot(scaled, scaled.T, precision=lax.Precision.HIGHEST)
    lower = jnp.linalg.cholesky(gram / total)
    scores = lax.linalg.triangular_solve(lower, scaled, left_side=True, lower=True)
    return (lower.T, scores)
```

```python
import functools
import jax
import jax.numpy as jnp
from jax import lax
from jax.experimental import pallas as pl
from jax.experimental.pallas import tpu as pltpu
from jax.sharding import PartitionSpec as P

MESH = pl.DeviceIdType.MESH
CHUNKS = 4


def gather_gram(n_band, n_dev, anomaly, area, mask, own_area, own_mask, hi_out, lo_out, gram_out,
                land, hi, lo, hh, hl, part, piece_in, zsend, zin, agsend, gsum,
                load_sem, a2a_send, a2a_recv, rs_send, rs_recv, z_send, z_recv, ag_send, ag_recv, out_sem):
    z = lax.axis_index("band")
    me = lax.axis_index("dev")
    snaps, cells = land.shape
    rows = snaps // n_dev
    width = cells // CHUNKS

    barrier = pltpu.get_barrier_semaphore()

    def greet(i, _):
        pl.semaphore_signal(barrier, inc=1, device_id=(z, lax.rem(me + i, n_dev)), device_id_type=MESH)
        return _

    def greet_z(i, _):
        pl.semaphore_signal(barrier, inc=1, device_id=(lax.rem(z + i, n_band), me), device_id_type=MESH)
        return _

    lax.fori_loop(1, n_dev, greet, 0)
    lax.fori_loop(1, n_band, greet_z, 0)
    own = pltpu.make_async_copy(anomaly.at[:, pl.ds(pl.multiple_of(me * cells, cells), cells)],
                                land.at[pl.ds(pl.multiple_of(me * rows, rows), rows), :], load_sem)
    own.start()
    pl.semaphore_wait(barrier, n_dev - 1 + n_band - 1)

    for c in range(CHUNKS):
        def send(i, _, c=c):
            to = lax.rem(me + i, n_dev)
            pltpu.make_async_remote_copy(
                src_ref=anomaly.at[:, pl.ds(pl.multiple_of(to * cells + c * width, width), width)],
                dst_ref=land.at[pl.ds(pl.multiple_of(me * rows, rows), rows), pl.ds(c * width, width)],
                send_sem=a2a_send.at[c], recv_sem=a2a_recv.at[c],
                device_id=(z, to), device_id_type=MESH).start()
            return _
        lax.fori_loop(1, n_dev, send, 0)

    band_total = jnp.sum(area[...] * mask[...].astype(jnp.float32))
    root = jnp.sqrt(own_area[...] * own_mask[...].astype(jnp.float32))
    hh[...] = jnp.zeros_like(hh)
    hl[...] = jnp.zeros_like(hl)
    own.wait()
    nt = (((1,), (1,)), ((), ()))
    for c in range(CHUNKS):
        window = land.at[pl.ds(0, rows * (n_dev - 1)), pl.ds(c * width, width)]
        pltpu.make_async_copy(window, window, a2a_recv.at[c]).wait()
        for t in range(width // 128):
            k = c * (width // 128) + t
            at = pl.ds(k * 128, 128)
            x = land[:, at] * root[k:k + 1, :]
            top = x.astype(jnp.bfloat16)
            hi[:, at] = top
            lo[:, at] = (x - top.astype(jnp.float32)).astype(jnp.bfloat16)
        at = pl.ds(c * width, width)
        hh[...] += lax.dot_general(hi[:, at], hi[:, at], nt, preferred_element_type=jnp.float32)
        hl[...] += lax.dot_general(hi[:, at], lo[:, at], nt, preferred_element_type=jnp.float32)
    put_hi = pltpu.make_async_copy(hi, hi_out, out_sem.at[0])
    put_lo = pltpu.make_async_copy(lo, lo_out, out_sem.at[1])
    put_hi.start()
    put_lo.start()
    part[...] = (hh[...] + (hl[...] + hl[...].T)).reshape(n_dev, rows, snaps)

    def send_piece(i, _):
        to = lax.rem(me + i, n_dev)
        pltpu.make_async_remote_copy(
            src_ref=part.at[to], dst_ref=piece_in.at[me], send_sem=rs_send, recv_sem=rs_recv,
            device_id=(z, to), device_id_type=MESH).start()
        return _
    lax.fori_loop(1, n_dev, send_piece, 0)
    piece_in[me] = part[me]
    some = piece_in.at[pl.ds(0, n_dev - 1)]
    pltpu.make_async_copy(some, some, rs_recv).wait()
    piece = jnp.sum(piece_in[...], axis=0)

    zsend[:, :snaps] = piece
    zsend[:, snaps:] = jnp.full((rows, 128), band_total, jnp.float32)
    zin[z] = zsend[...]

    def send_z(i, _):
        pltpu.make_async_remote_copy(
            src_ref=zsend, dst_ref=zin.at[z], send_sem=z_send, recv_sem=z_recv,
            device_id=(lax.rem(z + i, n_band), me), device_id_type=MESH).start()
        return _
    lax.fori_loop(1, n_band, send_z, 0)
    some_z = zin.at[pl.ds(0, n_band - 1)]
    pltpu.make_async_copy(some_z, some_z, z_recv).wait()
    summed = jnp.sum(zin[...], axis=0)
    total = summed[:, snaps:]
    agsend[...] = summed[:, :snaps] / jnp.concatenate([total, total], axis=1)
    gsum[me] = agsend[...]

    def send_sum(i, _):
        pltpu.make_async_remote_copy(
            src_ref=agsend, dst_ref=gsum.at[me], send_sem=ag_send, recv_sem=ag_recv,
            device_id=(z, lax.rem(me + i, n_dev)), device_id_type=MESH).start()
        return _
    lax.fori_loop(1, n_dev, send_sum, 0)
    some_g = gsum.at[pl.ds(0, n_dev - 1)]
    pltpu.make_async_copy(some_g, some_g, ag_recv).wait()
    gram_out[...] = gsum[...].reshape(snaps, snaps)
    pltpu.make_async_copy(some, some, rs_send).wait()
    pltpu.make_async_copy(some_z, some_z, z_send).wait()
    pltpu.make_async_copy(some_g, some_g, ag_send).wait()
    for c in range(CHUNKS):
        window = land.at[pl.ds(0, rows * (n_dev - 1)), pl.ds(c * width, width)]
        pltpu.make_async_copy(window, window, a2a_send.at[c]).wait()
    put_hi.wait()
    put_lo.wait()


def call_gather_gram(mesh, anomaly, ocean_mask, area_weight):
    n_band, n_dev = mesh.shape["band"], mesh.shape["dev"]
    rows, band_cells = anomaly.shape
    snaps, cells = rows * n_dev, band_cells // n_dev
    area2 = area_weight.reshape(band_cells // 128, 128)
    mask2 = ocean_mask.reshape(band_cells // 128, 128)
    at = lax.axis_index("dev") * (cells // 128)
    own_area = lax.dynamic_slice_in_dim(area2, at, cells // 128, 0)
    own_mask = lax.dynamic_slice_in_dim(mask2, at, cells // 128, 0)
    f32, bf16 = jnp.float32, jnp.bfloat16
    vmem = pl.BlockSpec(memory_space=pltpu.VMEM)
    hbm = pl.BlockSpec(memory_space=pl.ANY)
    dma = pltpu.SemaphoreType.DMA
    return pl.pallas_call(
        functools.partial(gather_gram, n_band, n_dev),
        name="gather_gram",
        out_shape=(jax.ShapeDtypeStruct((snaps, cells), bf16), jax.ShapeDtypeStruct((snaps, cells), bf16),
                   jax.ShapeDtypeStruct((snaps, snaps), f32)),
        in_specs=[hbm, vmem, vmem, vmem, vmem],
        out_specs=(hbm, hbm, vmem),
        scratch_shapes=[
            pltpu.VMEM((snaps, cells), f32), pltpu.VMEM((snaps, cells), bf16), pltpu.VMEM((snaps, cells), bf16),
            pltpu.VMEM((snaps, snaps), f32), pltpu.VMEM((snaps, snaps), f32),
            pltpu.VMEM((n_dev, rows, snaps), f32), pltpu.VMEM((n_dev, rows, snaps), f32),
            pltpu.VMEM((rows, snaps + 128), f32), pltpu.VMEM((n_band, rows, snaps + 128), f32),
            pltpu.VMEM((rows, snaps), f32), pltpu.VMEM((n_dev, rows, snaps), f32),
            dma, dma((CHUNKS,)), dma((CHUNKS,)), dma, dma, dma, dma, dma, dma, dma((2,)),
        ],
        compiler_params=pltpu.CompilerParams(collective_id=0, has_side_effects=True, vmem_limit_bytes=40 * 1024 * 1024),
        cost_estimate=pl.CostEstimate(flops=4 * snaps * snaps * cells, bytes_accessed=8 * snaps * cells, transcendentals=0),
    )(anomaly, area2, mask2, own_area, own_mask)


def solution(mesh):
    def on_device(anomaly, ocean_mask, area_weight):
        hi, lo, gram = call_gather_gram(mesh, anomaly, ocean_mask, area_weight)
        lower = jnp.linalg.cholesky(gram)
        scaled = hi.astype(jnp.float32) + lo.astype(jnp.float32)
        scores = lax.linalg.triangular_solve(lower, scaled, left_side=True, lower=True)
        return (lower.T, scores)

    return jax.shard_map(
        on_device,
        mesh=mesh,
        in_specs=(P("dev", "band"), P("band"), P("band")),
        out_specs=(P(), P(None, ("band", "dev"))),
        check_vma=False,
    )
```

```python
import functools
import jax
import jax.numpy as jnp
from jax import lax
from jax.experimental import pallas as pl
from jax.experimental.pallas import tpu as pltpu
from jax.sharding import PartitionSpec as P

MESH = pl.DeviceIdType.MESH
CHUNKS = 4


def gather_gram(n_band, n_dev, anomaly, area_hbm, mask_hbm, hi_out, lo_out, gram_out,
                area, mask, land, hi, lo, hh, hl, part, piece_in, zsend, zin, agsend, gsum,
                load_sem, area_sem, mask_sem, a2a_send, a2a_recv, rs_send, rs_recv, z_send, z_recv, ag_send, ag_recv, out_sem):
    z = lax.axis_index("band")
    me = lax.axis_index("dev")
    snaps, cells = land.shape
    rows = snaps // n_dev
    width = cells // CHUNKS

    barrier = pltpu.get_barrier_semaphore()

    def greet(i, _):
        pl.semaphore_signal(barrier, inc=1, device_id=(z, lax.rem(me + i, n_dev)), device_id_type=MESH)
        return _

    def greet_z(i, _):
        pl.semaphore_signal(barrier, inc=1, device_id=(lax.rem(z + i, n_band), me), device_id_type=MESH)
        return _

    lax.fori_loop(1, n_dev, greet, 0)
    lax.fori_loop(1, n_band, greet_z, 0)
    own = pltpu.make_async_copy(anomaly.at[:, pl.ds(pl.multiple_of(me * cells, cells), cells)],
                                land.at[pl.ds(pl.multiple_of(me * rows, rows), rows), :], load_sem)
    own.start()
    get_area = pltpu.make_async_copy(area_hbm, area, area_sem)
    get_mask = pltpu.make_async_copy(mask_hbm, mask, mask_sem)
    get_area.start()
    get_mask.start()
    pl.semaphore_wait(barrier, n_dev - 1 + n_band - 1)

    for c in range(CHUNKS):
        def send(i, _, c=c):
            to = lax.rem(me + i, n_dev)
            pltpu.make_async_remote_copy(
                src_ref=anomaly.at[:, pl.ds(pl.multiple_of(to * cells + c * width, width), width)],
                dst_ref=land.at[pl.ds(pl.multiple_of(me * rows, rows), rows), pl.ds(c * width, width)],
                send_sem=a2a_send.at[c], recv_sem=a2a_recv.at[c],
                device_id=(z, to), device_id_type=MESH).start()
            return _
        lax.fori_loop(1, n_dev, send, 0)

    get_area.wait()
    get_mask.wait()
    band_total = jnp.sum(area[...] * mask[...].astype(jnp.float32))
    mine = pl.ds(pl.multiple_of(me * (cells // 128), 8), cells // 128)
    root = jnp.sqrt(area[mine, :] * mask[mine, :].astype(jnp.float32))
    hh[...] = jnp.zeros_like(hh)
    hl[...] = jnp.zeros_like(hl)
    own.wait()
    nt = (((1,), (1,)), ((), ()))
    for c in range(CHUNKS):
        window = land.at[pl.ds(0, rows * (n_dev - 1)), pl.ds(c * width, width)]
        pltpu.make_async_copy(window, window, a2a_recv.at[c]).wait()
        for t in range(width // 128):
            k = c * (width // 128) + t
            at = pl.ds(k * 128, 128)
            x = land[:, at] * root[k:k + 1, :]
            top = x.astype(jnp.bfloat16)
            hi[:, at] = top
            lo[:, at] = (x - top.astype(jnp.float32)).astype(jnp.bfloat16)
        at = pl.ds(c * width, width)
        hh[...] += lax.dot_general(hi[:, at], hi[:, at], nt, preferred_element_type=jnp.float32)
        hl[...] += lax.dot_general(hi[:, at], lo[:, at], nt, preferred_element_type=jnp.float32)
    put_hi = pltpu.make_async_copy(hi, hi_out, out_sem.at[0])
    put_lo = pltpu.make_async_copy(lo, lo_out, out_sem.at[1])
    put_hi.start()
    put_lo.start()
    part[...] = (hh[...] + (hl[...] + hl[...].T)).reshape(n_dev, rows, snaps)

    def send_piece(i, _):
        to = lax.rem(me + i, n_dev)
        pltpu.make_async_remote_copy(
            src_ref=part.at[to], dst_ref=piece_in.at[me], send_sem=rs_send, recv_sem=rs_recv,
            device_id=(z, to), device_id_type=MESH).start()
        return _
    lax.fori_loop(1, n_dev, send_piece, 0)
    piece_in[me] = part[me]
    some = piece_in.at[pl.ds(0, n_dev - 1)]
    pltpu.make_async_copy(some, some, rs_recv).wait()
    piece = jnp.sum(piece_in[...], axis=0)

    zsend[:, :snaps] = piece
    zsend[:, snaps:] = jnp.full((rows, 128), band_total, jnp.float32)
    zin[z] = zsend[...]

    def send_z(i, _):
        pltpu.make_async_remote_copy(
            src_ref=zsend, dst_ref=zin.at[z], send_sem=z_send, recv_sem=z_recv,
            device_id=(lax.rem(z + i, n_band), me), device_id_type=MESH).start()
        return _
    lax.fori_loop(1, n_band, send_z, 0)
    some_z = zin.at[pl.ds(0, n_band - 1)]
    pltpu.make_async_copy(some_z, some_z, z_recv).wait()
    summed = jnp.sum(zin[...], axis=0)
    total = summed[:, snaps:]
    agsend[...] = summed[:, :snaps] / jnp.concatenate([total, total], axis=1)
    gsum[me] = agsend[...]

    def send_sum(i, _):
        pltpu.make_async_remote_copy(
            src_ref=agsend, dst_ref=gsum.at[me], send_sem=ag_send, recv_sem=ag_recv,
            device_id=(z, lax.rem(me + i, n_dev)), device_id_type=MESH).start()
        return _
    lax.fori_loop(1, n_dev, send_sum, 0)
    some_g = gsum.at[pl.ds(0, n_dev - 1)]
    pltpu.make_async_copy(some_g, some_g, ag_recv).wait()
    gram_out[...] = gsum[...].reshape(snaps, snaps)
    pltpu.make_async_copy(some, some, rs_send).wait()
    pltpu.make_async_copy(some_z, some_z, z_send).wait()
    pltpu.make_async_copy(some_g, some_g, ag_send).wait()
    for c in range(CHUNKS):
        window = land.at[pl.ds(0, rows * (n_dev - 1)), pl.ds(c * width, width)]
        pltpu.make_async_copy(window, window, a2a_send.at[c]).wait()
    put_hi.wait()
    put_lo.wait()


def call_gather_gram(mesh, anomaly, ocean_mask, area_weight):
    n_band, n_dev = mesh.shape["band"], mesh.shape["dev"]
    rows, band_cells = anomaly.shape
    snaps, cells = rows * n_dev, band_cells // n_dev
    area2 = area_weight.reshape(band_cells // 128, 128)
    mask2 = ocean_mask.reshape(band_cells // 128, 128)
    f32, bf16 = jnp.float32, jnp.bfloat16
    vmem = pl.BlockSpec(memory_space=pltpu.VMEM)
    hbm = pl.BlockSpec(memory_space=pl.ANY)
    dma = pltpu.SemaphoreType.DMA
    return pl.pallas_call(
        functools.partial(gather_gram, n_band, n_dev),
        name="gather_gram",
        out_shape=(jax.ShapeDtypeStruct((snaps, cells), bf16), jax.ShapeDtypeStruct((snaps, cells), bf16),
                   jax.ShapeDtypeStruct((snaps, snaps), f32)),
        in_specs=[hbm, hbm, hbm],
        out_specs=(hbm, hbm, vmem),
        scratch_shapes=[
            pltpu.VMEM((band_cells // 128, 128), f32), pltpu.VMEM((band_cells // 128, 128), jnp.int32),
            pltpu.VMEM((snaps, cells), f32), pltpu.VMEM((snaps, cells), bf16), pltpu.VMEM((snaps, cells), bf16),
            pltpu.VMEM((snaps, snaps), f32), pltpu.VMEM((snaps, snaps), f32),
            pltpu.VMEM((n_dev, rows, snaps), f32), pltpu.VMEM((n_dev, rows, snaps), f32),
            pltpu.VMEM((rows, snaps + 128), f32), pltpu.VMEM((n_band, rows, snaps + 128), f32),
            pltpu.VMEM((rows, snaps), f32), pltpu.VMEM((n_dev, rows, snaps), f32),
            dma, dma, dma, dma((CHUNKS,)), dma((CHUNKS,)), dma, dma, dma, dma, dma, dma, dma((2,)),
        ],
        compiler_params=pltpu.CompilerParams(collective_id=0, has_side_effects=True, vmem_limit_bytes=40 * 1024 * 1024),
        cost_estimate=pl.CostEstimate(flops=4 * snaps * snaps * cells, bytes_accessed=8 * snaps * cells, transcendentals=0),
    )(anomaly, area2, mask2)


PANEL = 16
TN = (((0,), (0,)), ((), ()))


def split3(x):
    a = x.astype(jnp.bfloat16)
    rest = x - a.astype(jnp.float32)
    b = rest.astype(jnp.bfloat16)
    return a, b, (rest - b.astype(jnp.float32)).astype(jnp.bfloat16)


def factor(work, upper, inverse):
    n = work.shape[0]
    row = lax.broadcasted_iota(jnp.int32, (8, 128), 0)
    lane = lax.broadcasted_iota(jnp.int32, (8, 128), 1)
    groups = PANEL // 8
    tiles = n // 128
    for k in range(n // PANEL):
        base = k * PANEL
        home, off = base // 128, base % 128
        more = base + PANEL < n
        inside = (lane >= off) & (lane < off + PANEL)
        count = 2 * groups if more else groups
        panel = [[work[base + 8 * s:base + 8 * s + 8, t * 128:(t + 1) * 128] for t in range(tiles)] for s in range(count)]
        cols = [[jnp.broadcast_to(panel[s][home][:, off + c:off + c + 1], (8, 128)) for s in range(count)] for c in range(PANEL)]
        diag = [panel[s][home] for s in range(groups)]
        for s in range(count):
            unit = jnp.where(lane == row + (off + 8 * s), 1.0, 0.0) if s < groups else 0.0
            panel[s][home] = jnp.where(inside, unit, panel[s][home])
        pivots = [None] * groups
        for j in range(PANEL):
            own, r = j // 8, j % 8
            pivot = jnp.broadcast_to(cols[j][own][r:r + 1, :], (8, 128))
            pivots[own] = pivot if r == 0 else jnp.where(row >= r, pivot, pivots[own])
            inv = 1.0 / pivot
            first = own if r < 7 else own + 1
            mult = {}
            for s in range(first, count):
                m = jnp.where(row > r, cols[j][s], 0.0) if s == own else cols[j][s]
                mult[s] = m * inv
            for c in range(j + 1, PANEL):
                line = jnp.broadcast_to(cols[c][own][r:r + 1, :], (8, 128))
                for s in range(first, count):
                    if s >= groups or 8 * s + 7 > j:
                        cols[c][s] = cols[c][s] - mult[s] * line
            for t in range(tiles):
                line = jnp.broadcast_to(panel[own][t][r:r + 1, :], (8, 128))
                for s in range(first, count):
                    panel[s][t] = panel[s][t] - mult[s] * line
            line = jnp.broadcast_to(diag[own][r:r + 1, :], (8, 128))
            for s in range(first, groups):
                diag[s] = diag[s] - mult[s] * line
        for s in range(groups):
            scale = lax.rsqrt(pivots[s])
            at = pl.ds(base + 8 * s, 8)
            for t in range(tiles):
                val = panel[s][t] * scale
                panel[s][t] = val
                wide = pl.ds(t * 128, 128)
                if t < home:
                    inverse[at, wide] = val
                    upper[at, wide] = jnp.zeros((8, 128), jnp.float32)
                elif t > home:
                    inverse[at, wide] = jnp.zeros((8, 128), jnp.float32)
                    upper[at, wide] = val
                else:
                    inverse[at, wide] = jnp.where(lane <= row + (off + 8 * s), val, 0.0)
                    u = jnp.where(inside, diag[s] * scale, val)
                    upper[at, wide] = jnp.where(lane >= row + (off + 8 * s), u, 0.0)
        if more:
            for s in range(groups, count):
                for t in range(tiles):
                    work[base + 8 * s:base + 8 * s + 8, t * 128:(t + 1) * 128] = panel[s][t]
        far = base + 2 * PANEL
        if far < n:
            lines = jnp.concatenate([jnp.concatenate(panel[s], axis=1) for s in range(groups)], axis=0)
            a, b, c = split3(lines)
            left = jnp.concatenate([a, a, b, a, b, c], axis=0)
            right = jnp.concatenate([a, b, a, c, b, a], axis=0)
            start = far // 128 * 128
            delta = lax.dot_general(left[:, start:], right, TN, preferred_element_type=jnp.float32)
            for i in range(far, n, 8):
                for t in range(tiles):
                    at, wide = slice(i, i + 8), slice(t * 128, (t + 1) * 128)
                    old = work[at, wide]
                    if t == home:
                        old = jnp.where(inside, 0.0, old)
                    work[at, wide] = old - delta[i - start:i - start + 8, wide]


def solve(gram, hi_in, lo_in, upper, scores, work, inverse, hi, lo, out, in_sem, out_sem):
    get_hi = pltpu.make_async_copy(hi_in, hi, in_sem.at[0])
    get_lo = pltpu.make_async_copy(lo_in, lo, in_sem.at[1])
    get_hi.start()
    get_lo.start()
    work[...] = gram[...]
    factor(work, upper, inverse)
    full = inverse[...]
    top = full.astype(jnp.bfloat16)
    rest = (full - top.astype(jnp.float32)).astype(jnp.bfloat16)
    get_hi.wait()
    get_lo.wait()
    width = 512
    puts = []
    for c in range(hi.shape[1] // width):
        at = pl.ds(c * width, width)
        a, b = hi[:, at], lo[:, at]
        out[:, at] = (jnp.dot(top, a, preferred_element_type=jnp.float32)
                      + (jnp.dot(top, b, preferred_element_type=jnp.float32)
                         + jnp.dot(rest, a, preferred_element_type=jnp.float32)))
        put = pltpu.make_async_copy(out.at[:, at], scores.at[:, at], out_sem.at[c])
        put.start()
        puts.append(put)
    for put in puts:
        put.wait()


def call_solve(gram, hi, lo):
    snaps, cells = hi.shape
    f32, bf16 = jnp.float32, jnp.bfloat16
    vmem = pl.BlockSpec(memory_space=pltpu.VMEM)
    hbm = pl.BlockSpec(memory_space=pl.ANY)
    dma = pltpu.SemaphoreType.DMA
    return pl.pallas_call(
        solve,
        name="solve",
        out_shape=(jax.ShapeDtypeStruct((snaps, snaps), f32), jax.ShapeDtypeStruct((snaps, cells), f32)),
        in_specs=[vmem, hbm, hbm],
        out_specs=(vmem, hbm),
        scratch_shapes=[pltpu.VMEM((snaps, snaps), f32), pltpu.VMEM((snaps, snaps), f32),
                        pltpu.VMEM((snaps, cells), bf16), pltpu.VMEM((snaps, cells), bf16),
                        pltpu.VMEM((snaps, cells), f32), dma((2,)), dma((cells // 512,))],
        compiler_params=pltpu.CompilerParams(vmem_limit_bytes=40 * 1024 * 1024),
        cost_estimate=pl.CostEstimate(flops=6 * snaps * snaps * cells, bytes_accessed=8 * snaps * cells, transcendentals=0),
    )(gram, hi, lo)


def solution(mesh):
    def on_device(anomaly, ocean_mask, area_weight):
        hi, lo, gram = call_gather_gram(mesh, anomaly, ocean_mask, area_weight)
        return call_solve(gram, hi, lo)

    return jax.shard_map(
        on_device,
        mesh=mesh,
        in_specs=(P("dev", "band"), P("band"), P("band")),
        out_specs=(P(), P(None, ("band", "dev"))),
        check_vma=False,
    )
```

```python
import functools
import jax
import jax.numpy as jnp
from jax import lax
from jax.experimental import pallas as pl
from jax.experimental.pallas import tpu as pltpu
from jax.sharding import PartitionSpec as P

MESH = pl.DeviceIdType.MESH
CHUNKS = 8
SIDE = 4


def ring(d, n):
    return min(d, n - d)


AROUND = sorted(((dx, dy, dc) for dx in range(SIDE) for dy in range(SIDE) for dc in range(2) if dx or dy or dc),
                key=lambda o: -(ring(o[0], SIDE) + ring(o[1], SIDE)))


def gather_gram(n_band, n_dev, anomaly, area_hbm, mask_hbm, hi_out, lo_out, gram_out,
                area, mask, land, hi, lo, hh, part, piece_in, zsend, zin, agsend, gsum,
                load_sem, area_sem, mask_sem, a2a_send, a2a_recv, rs_send, rs_recv, z_send, z_recv, ag_send, ag_recv, out_sem):
    z = lax.axis_index("band")
    me = lax.axis_index("dev")
    x, y, core = me // (2 * SIDE), lax.rem(me, 2 * SIDE) // 2, lax.rem(me, 2)
    peers = [lax.rem(x + dx, SIDE) * (2 * SIDE) + lax.rem(y + dy, SIDE) * 2 + lax.rem(core + dc, 2) for dx, dy, dc in AROUND]
    levels = [lax.rem(z + dz, n_band) for dz in sorted(range(1, n_band), key=lambda d: -ring(d, n_band))]
    snaps, cells = land.shape
    rows = snaps // n_dev
    width = cells // CHUNKS

    barrier = pltpu.get_barrier_semaphore()

    for to in peers:
        pl.semaphore_signal(barrier, inc=1, device_id=(z, to), device_id_type=MESH)
    for to in levels:
        pl.semaphore_signal(barrier, inc=1, device_id=(to, me), device_id_type=MESH)
    own = pltpu.make_async_copy(anomaly.at[:, pl.ds(pl.multiple_of(me * cells, cells), cells)],
                                land.at[pl.ds(pl.multiple_of(me * rows, rows), rows), :], load_sem)
    own.start()
    get_area = pltpu.make_async_copy(area_hbm, area, area_sem)
    get_mask = pltpu.make_async_copy(mask_hbm, mask, mask_sem)
    get_area.start()
    get_mask.start()
    pl.semaphore_wait(barrier, n_dev - 1 + n_band - 1)

    def send_chunk(c, _):
        column = pl.multiple_of(c * width, width)
        for to in peers:
            pltpu.make_async_remote_copy(
                src_ref=anomaly.at[:, pl.ds(pl.multiple_of(to * cells + column, width), width)],
                dst_ref=land.at[pl.ds(pl.multiple_of(me * rows, rows), rows), pl.ds(column, width)],
                send_sem=a2a_send.at[c], recv_sem=a2a_recv.at[c],
                device_id=(z, to), device_id_type=MESH).start()
        return _
    lax.fori_loop(0, CHUNKS, send_chunk, 0)

    get_area.wait()
    get_mask.wait()
    band_total = jnp.sum(area[...] * mask[...].astype(jnp.float32))
    mine = pl.ds(pl.multiple_of(me * (cells // 128), 8), cells // 128)
    root = jnp.sqrt(area[mine, :] * mask[mine, :].astype(jnp.float32))
    hh[...] = jnp.zeros_like(hh)
    own.wait()
    nt = (((1,), (1,)), ((), ()))
    for c in range(CHUNKS):
        window = land.at[pl.ds(0, rows * (n_dev - 1)), pl.ds(c * width, width)]
        pltpu.make_async_copy(window, window, a2a_recv.at[c]).wait()
        for t in range(width // 128):
            k = c * (width // 128) + t
            at = pl.ds(k * 128, 128)
            x = land[:, at] * root[k:k + 1, :]
            top = x.astype(jnp.bfloat16)
            hi[:, at] = top
            lo[:, at] = (x - top.astype(jnp.float32)).astype(jnp.bfloat16)
        at = pl.ds(c * width, width)
        a, b = hi[:, at], lo[:, at]
        hh[...] += (lax.dot_general(a, a, nt, preferred_element_type=jnp.float32)
                    + (lax.dot_general(a, b, nt, preferred_element_type=jnp.float32)
                       + lax.dot_general(b, a, nt, preferred_element_type=jnp.float32)))
    put_hi = pltpu.make_async_copy(hi, hi_out, out_sem.at[0])
    put_lo = pltpu.make_async_copy(lo, lo_out, out_sem.at[1])
    part[...] = hh[...].reshape(n_dev, rows, snaps)

    for to in peers:
        pltpu.make_async_remote_copy(
            src_ref=part.at[to], dst_ref=piece_in.at[me], send_sem=rs_send, recv_sem=rs_recv,
            device_id=(z, to), device_id_type=MESH).start()
    piece_in[me] = part[me]
    put_hi.start()
    put_lo.start()
    some = piece_in.at[pl.ds(0, n_dev - 1)]
    pltpu.make_async_copy(some, some, rs_recv).wait()
    piece = jnp.sum(piece_in[...], axis=0)

    zsend[:, :snaps] = piece
    zsend[:, snaps:] = jnp.full((rows, 128), band_total, jnp.float32)
    zin[z] = zsend[...]

    for to in levels:
        pltpu.make_async_remote_copy(
            src_ref=zsend, dst_ref=zin.at[z], send_sem=z_send, recv_sem=z_recv,
            device_id=(to, me), device_id_type=MESH).start()
    some_z = zin.at[pl.ds(0, n_band - 1)]
    pltpu.make_async_copy(some_z, some_z, z_recv).wait()
    summed = jnp.sum(zin[...], axis=0)
    total = summed[:, snaps:]
    agsend[...] = summed[:, :snaps] / jnp.concatenate([total, total], axis=1)
    gsum[me] = agsend[...]

    for to in peers:
        pltpu.make_async_remote_copy(
            src_ref=agsend, dst_ref=gsum.at[me], send_sem=ag_send, recv_sem=ag_recv,
            device_id=(z, to), device_id_type=MESH).start()
    some_g = gsum.at[pl.ds(0, n_dev - 1)]
    pltpu.make_async_copy(some_g, some_g, ag_recv).wait()
    gram_out[...] = gsum[...].reshape(snaps, snaps)
    pltpu.make_async_copy(some, some, rs_send).wait()
    pltpu.make_async_copy(some_z, some_z, z_send).wait()
    pltpu.make_async_copy(some_g, some_g, ag_send).wait()
    for c in range(CHUNKS):
        window = land.at[pl.ds(0, rows * (n_dev - 1)), pl.ds(c * width, width)]
        pltpu.make_async_copy(window, window, a2a_send.at[c]).wait()
    put_hi.wait()
    put_lo.wait()


def call_gather_gram(mesh, anomaly, ocean_mask, area_weight):
    n_band, n_dev = mesh.shape["band"], mesh.shape["dev"]
    rows, band_cells = anomaly.shape
    snaps, cells = rows * n_dev, band_cells // n_dev
    area2 = area_weight.reshape(band_cells // 128, 128)
    mask2 = ocean_mask.reshape(band_cells // 128, 128)
    f32, bf16 = jnp.float32, jnp.bfloat16
    vmem = pl.BlockSpec(memory_space=pltpu.VMEM)
    hbm = pl.BlockSpec(memory_space=pltpu.HBM)
    dma = pltpu.SemaphoreType.DMA
    return pl.pallas_call(
        functools.partial(gather_gram, n_band, n_dev),
        name="gather_gram",
        out_shape=(jax.ShapeDtypeStruct((snaps, cells), bf16), jax.ShapeDtypeStruct((snaps, cells), bf16),
                   jax.ShapeDtypeStruct((snaps, snaps), f32)),
        in_specs=[hbm, hbm, hbm],
        out_specs=(hbm, hbm, vmem),
        scratch_shapes=[
            pltpu.VMEM((band_cells // 128, 128), f32), pltpu.VMEM((band_cells // 128, 128), jnp.int32),
            pltpu.VMEM((snaps, cells), f32), pltpu.VMEM((snaps, cells), bf16), pltpu.VMEM((snaps, cells), bf16),
            pltpu.VMEM((snaps, snaps), f32),
            pltpu.VMEM((n_dev, rows, snaps), f32), pltpu.VMEM((n_dev, rows, snaps), f32),
            pltpu.VMEM((rows, snaps + 128), f32), pltpu.VMEM((n_band, rows, snaps + 128), f32),
            pltpu.VMEM((rows, snaps), f32), pltpu.VMEM((n_dev, rows, snaps), f32),
            dma, dma, dma, dma((CHUNKS,)), dma((CHUNKS,)), dma, dma, dma, dma, dma, dma, dma((2,)),
        ],
        compiler_params=pltpu.CompilerParams(collective_id=0, has_side_effects=True, vmem_limit_bytes=40 * 1024 * 1024),
        cost_estimate=pl.CostEstimate(flops=4 * snaps * snaps * cells, bytes_accessed=8 * snaps * cells, transcendentals=0),
    )(*[pltpu.with_memory_space_constraint(v, pltpu.HBM) for v in (anomaly, area2, mask2)])


PANEL = 16
TN = (((0,), (0,)), ((), ()))


def split3(x):
    a = x.astype(jnp.bfloat16)
    rest = x - a.astype(jnp.float32)
    b = rest.astype(jnp.bfloat16)
    return a, b, (rest - b.astype(jnp.float32)).astype(jnp.bfloat16)


def factor(work, upper, inverse):
    n = work.shape[0]
    row = lax.broadcasted_iota(jnp.int32, (8, 128), 0)
    lane = lax.broadcasted_iota(jnp.int32, (8, 128), 1)
    groups = PANEL // 8
    tiles = n // 128
    for k in range(n // PANEL):
        base = k * PANEL
        home, off = base // 128, base % 128
        more = base + PANEL < n
        inside = (lane >= off) & (lane < off + PANEL)
        count = 2 * groups if more else groups
        panel = [[work[base + 8 * s:base + 8 * s + 8, t * 128:(t + 1) * 128] for t in range(tiles)] for s in range(count)]
        cols = [[jnp.broadcast_to(panel[s][home][:, off + c:off + c + 1], (8, 128)) for s in range(count)] for c in range(PANEL)]
        diag = [panel[s][home] for s in range(groups)]
        for s in range(count):
            unit = jnp.where(lane == row + (off + 8 * s), 1.0, 0.0) if s < groups else 0.0
            panel[s][home] = jnp.where(inside, unit, panel[s][home])
        pivots = [None] * groups
        for j in range(PANEL):
            own, r = j // 8, j % 8
            pivot = jnp.broadcast_to(cols[j][own][r:r + 1, :], (8, 128))
            pivots[own] = pivot if r == 0 else jnp.where(row >= r, pivot, pivots[own])
            inv = 1.0 / pivot
            first = own if r < 7 else own + 1
            mult = {}
            for s in range(first, count):
                m = jnp.where(row > r, cols[j][s], 0.0) if s == own else cols[j][s]
                mult[s] = m * inv
            for c in range(j + 1, PANEL):
                line = jnp.broadcast_to(cols[c][own][r:r + 1, :], (8, 128))
                for s in range(first, count):
                    if s >= groups or 8 * s + 7 > j:
                        cols[c][s] = cols[c][s] - mult[s] * line
            for t in range(tiles):
                line = jnp.broadcast_to(panel[own][t][r:r + 1, :], (8, 128))
                for s in range(first, count):
                    panel[s][t] = panel[s][t] - mult[s] * line
            line = jnp.broadcast_to(diag[own][r:r + 1, :], (8, 128))
            for s in range(first, groups):
                diag[s] = diag[s] - mult[s] * line
        for s in range(groups):
            scale = lax.rsqrt(pivots[s])
            at = pl.ds(base + 8 * s, 8)
            for t in range(tiles):
                val = panel[s][t] * scale
                panel[s][t] = val
                wide = pl.ds(t * 128, 128)
                if t < home:
                    inverse[at, wide] = val
                    upper[at, wide] = jnp.zeros((8, 128), jnp.float32)
                elif t > home:
                    inverse[at, wide] = jnp.zeros((8, 128), jnp.float32)
                    upper[at, wide] = val
                else:
                    inverse[at, wide] = jnp.where(lane <= row + (off + 8 * s), val, 0.0)
                    u = jnp.where(inside, diag[s] * scale, val)
                    upper[at, wide] = jnp.where(lane >= row + (off + 8 * s), u, 0.0)
        if more:
            for s in range(groups, count):
                for t in range(tiles):
                    work[base + 8 * s:base + 8 * s + 8, t * 128:(t + 1) * 128] = panel[s][t]
        far = base + 2 * PANEL
        if far < n:
            lines = jnp.concatenate([jnp.concatenate(panel[s], axis=1) for s in range(groups)], axis=0)
            a, b, c = split3(lines)
            left = jnp.concatenate([a, a, b, a, b, c], axis=0)
            right = jnp.concatenate([a, b, a, c, b, a], axis=0)
            start = far // 128 * 128
            delta = lax.dot_general(left[:, start:], right, TN, preferred_element_type=jnp.float32)
            for i in range(far, n, 8):
                for t in range(tiles):
                    at, wide = slice(i, i + 8), slice(t * 128, (t + 1) * 128)
                    old = work[at, wide]
                    if t == home:
                        old = jnp.where(inside, 0.0, old)
                    work[at, wide] = old - delta[i - start:i - start + 8, wide]


def solve(gram, hi_in, lo_in, upper, scores, work, inverse, hi, lo, out, in_sem, out_sem):
    get_hi = pltpu.make_async_copy(hi_in, hi, in_sem.at[0])
    get_lo = pltpu.make_async_copy(lo_in, lo, in_sem.at[1])
    get_hi.start()
    get_lo.start()
    work[...] = gram[...]
    factor(work, upper, inverse)
    full = inverse[...]
    top = full.astype(jnp.bfloat16)
    rest = (full - top.astype(jnp.float32)).astype(jnp.bfloat16)
    get_hi.wait()
    get_lo.wait()
    width = 512
    puts = []
    for c in range(hi.shape[1] // width):
        at = pl.ds(c * width, width)
        a, b = hi[:, at], lo[:, at]
        out[:, at] = (jnp.dot(top, a, preferred_element_type=jnp.float32)
                      + (jnp.dot(top, b, preferred_element_type=jnp.float32)
                         + jnp.dot(rest, a, preferred_element_type=jnp.float32)))
        put = pltpu.make_async_copy(out.at[:, at], scores.at[:, at], out_sem.at[c])
        put.start()
        puts.append(put)
    for put in puts:
        put.wait()


def call_solve(gram, hi, lo):
    snaps, cells = hi.shape
    f32, bf16 = jnp.float32, jnp.bfloat16
    vmem = pl.BlockSpec(memory_space=pltpu.VMEM)
    hbm = pl.BlockSpec(memory_space=pltpu.HBM)
    dma = pltpu.SemaphoreType.DMA
    return pl.pallas_call(
        solve,
        name="solve",
        out_shape=(jax.ShapeDtypeStruct((snaps, snaps), f32), jax.ShapeDtypeStruct((snaps, cells), f32)),
        in_specs=[vmem, hbm, hbm],
        out_specs=(vmem, hbm),
        scratch_shapes=[pltpu.VMEM((snaps, snaps), f32), pltpu.VMEM((snaps, snaps), f32),
                        pltpu.VMEM((snaps, cells), bf16), pltpu.VMEM((snaps, cells), bf16),
                        pltpu.VMEM((snaps, cells), f32), dma((2,)), dma((cells // 512,))],
        compiler_params=pltpu.CompilerParams(vmem_limit_bytes=40 * 1024 * 1024),
        cost_estimate=pl.CostEstimate(flops=6 * snaps * snaps * cells, bytes_accessed=8 * snaps * cells, transcendentals=0),
    )(gram, hi, lo)


def solution(mesh):
    def on_device(anomaly, ocean_mask, area_weight):
        hi, lo, gram = call_gather_gram(mesh, anomaly, ocean_mask, area_weight)
        return call_solve(gram, hi, lo)

    return jax.shard_map(
        on_device,
        mesh=mesh,
        in_specs=(P("dev", "band"), P("band"), P("band")),
        out_specs=(P(), P(None, ("band", "dev"))),
        check_vma=False,
    )
```

```python
import functools
import jax
import jax.numpy as jnp
from jax import lax
from jax.experimental import pallas as pl
from jax.experimental.pallas import tpu as pltpu
from jax.sharding import PartitionSpec as P

MESH = pl.DeviceIdType.MESH
CHUNKS = 8
SIDE = 4


def ring(d, n):
    return min(d, n - d)


AROUND = sorted(((dx, dy, dc) for dx in range(SIDE) for dy in range(SIDE) for dc in range(2) if dx or dy or dc),
                key=lambda o: -(ring(o[0], SIDE) + ring(o[1], SIDE)))


def gather_gram(n_band, n_dev, anomaly, area_hbm, mask_hbm, hi_out, lo_out, packed_out,
                area, mask, land, hi, lo, gram, part, piece_in, extra_in, tsend, tin, zsend, zin, xsend, xin, agsend, gsum,
                load_sem, area_sem, mask_sem, a2a_send, a2a_recv, rs_send, rs_recv, t_send, t_recv, z_send, z_recv,
                ag_send, ag_recv, xr_send, xr_recv, xz_send, xz_recv, xa_send, xa_recv, out_sem):
    z = lax.axis_index("band")
    me = lax.axis_index("dev")
    x, y, core = me // (2 * SIDE), lax.rem(me, 2 * SIDE) // 2, lax.rem(me, 2)
    peers = [lax.rem(x + dx, SIDE) * (2 * SIDE) + lax.rem(y + dy, SIDE) * 2 + lax.rem(core + dc, 2) for dx, dy, dc in AROUND]
    levels = [lax.rem(z + dz, n_band) for dz in sorted(range(1, n_band), key=lambda d: -ring(d, n_band))]
    snaps, cells = land.shape
    rows = snaps // n_dev
    width = cells // CHUNKS

    barrier = pltpu.get_barrier_semaphore()

    for to in peers:
        pl.semaphore_signal(barrier, inc=1, device_id=(z, to), device_id_type=MESH)
    for to in levels:
        pl.semaphore_signal(barrier, inc=1, device_id=(to, me), device_id_type=MESH)
    own = pltpu.make_async_copy(anomaly.at[:, pl.ds(pl.multiple_of(me * cells, cells), cells)],
                                land.at[pl.ds(pl.multiple_of(me * rows, rows), rows), :], load_sem)
    own.start()
    get_area = pltpu.make_async_copy(area_hbm, area, area_sem)
    get_mask = pltpu.make_async_copy(mask_hbm, mask, mask_sem)
    get_area.start()
    get_mask.start()
    pl.semaphore_wait(barrier, n_dev - 1 + n_band - 1)

    def push(src, dst, send_sem, recv_sem, to):
        pltpu.make_async_remote_copy(src_ref=src, dst_ref=dst, send_sem=send_sem, recv_sem=recv_sem,
                                     device_id=to, device_id_type=MESH).start()

    def drain(ref, sem):
        pltpu.make_async_copy(ref, ref, sem).wait()

    def send_chunk(c, _):
        column = pl.multiple_of(c * width, width)
        for to in peers:
            pltpu.make_async_remote_copy(
                src_ref=anomaly.at[:, pl.ds(pl.multiple_of(to * cells + column, width), width)],
                dst_ref=land.at[pl.ds(pl.multiple_of(me * rows, rows), rows), pl.ds(column, width)],
                send_sem=a2a_send.at[c], recv_sem=a2a_recv.at[c],
                device_id=(z, to), device_id_type=MESH).start()
        return _
    lax.fori_loop(0, CHUNKS, send_chunk, 0)

    get_area.wait()
    get_mask.wait()
    band_total = jnp.sum(area[...] * mask[...].astype(jnp.float32))
    tsend[...] = jnp.full((rows, 128), band_total, jnp.float32)
    tin[z] = tsend[...]
    for to in levels:
        push(tsend, tin.at[z], t_send, t_recv, (to, me))
    mine = pl.ds(pl.multiple_of(me * (cells // 128), 8), cells // 128)
    root = jnp.sqrt(area[mine, :] * mask[mine, :].astype(jnp.float32))
    gram[...] = jnp.zeros_like(gram)
    own.wait()
    nt = (((1,), (1,)), ((), ()))
    for c in range(CHUNKS):
        window = land.at[pl.ds(0, rows * (n_dev - 1)), pl.ds(c * width, width)]
        pltpu.make_async_copy(window, window, a2a_recv.at[c]).wait()
        for t in range(width // 128):
            k = c * (width // 128) + t
            at = pl.ds(k * 128, 128)
            x = land[:, at] * root[k:k + 1, :]
            top = x.astype(jnp.bfloat16)
            hi[:, at] = top
            lo[:, at] = (x - top.astype(jnp.float32)).astype(jnp.bfloat16)
        at = pl.ds(c * width, width)
        a, b = hi[:, at], lo[:, at]
        gram[...] += (lax.dot_general(a, a, nt, preferred_element_type=jnp.float32)
                    + (lax.dot_general(a, b, nt, preferred_element_type=jnp.float32)
                       + lax.dot_general(b, a, nt, preferred_element_type=jnp.float32)))
    row = lax.broadcasted_iota(jnp.int32, (8, 128), 0)
    lane = lax.broadcasted_iota(jnp.int32, (8, 128), 1)
    half = snaps // 2
    tiles = half // 8
    extra = jnp.zeros((8, 128), jnp.float32)
    for p in range(tiles):
        corner = gram[half + 8 * p:half + 8 * p + 8, half:]
        part[p] = jnp.where(row + 8 * p <= lane, gram[8 * p:8 * p + 8, :half], corner)
        part[tiles + p] = gram[8 * p:8 * p + 8, half:]
        extra = jnp.where(row + 8 * p == lane, corner, extra)
    part[2 * tiles] = extra
    last = n_dev - 1

    for to in peers:
        push(part.at[to], piece_in.at[me], rs_send, rs_recv, (z, to))

    @pl.when(me != last)
    def _():
        push(part.at[n_dev], extra_in.at[me], xr_send, xr_recv, (z, last))

    piece_in[me] = part[me]
    put_hi = pltpu.make_async_copy(hi, hi_out, out_sem.at[0])
    put_lo = pltpu.make_async_copy(lo, lo_out, out_sem.at[1])
    put_hi.start()
    put_lo.start()
    drain(tin.at[pl.ds(0, n_band - 1)], t_recv)
    total = jnp.sum(tin[...], axis=0)
    some = piece_in.at[pl.ds(0, n_dev - 1)]
    some_z = zin.at[pl.ds(0, n_band - 1)]
    some_g = gsum.at[pl.ds(0, n_dev - 1)]
    drain(some, rs_recv)
    zsend[...] = jnp.sum(piece_in[...], axis=0)
    for to in levels:
        push(zsend, zin.at[z], z_send, z_recv, (to, me))
    zin[z] = zsend[...]

    @pl.when(me == last)
    def _():
        extra_in[last] = part[n_dev]
        drain(extra_in.at[pl.ds(0, n_dev - 1)], xr_recv)
        xsend[...] = jnp.sum(extra_in[...], axis=0)
        for to in levels:
            push(xsend, xin.at[z], xz_send, xz_recv, (to, me))
        xin[z] = xsend[...]

    drain(some_z, z_recv)
    agsend[0] = jnp.sum(zin[...], axis=0) / total
    for to in peers:
        push(agsend.at[0], gsum.at[me], ag_send, ag_recv, (z, to))
    gsum[me] = agsend[0]

    @pl.when(me == last)
    def _():
        drain(xin.at[pl.ds(0, n_band - 1)], xz_recv)
        agsend[1] = jnp.sum(xin[...], axis=0) / total
        for to in peers:
            push(agsend.at[1], gsum.at[n_dev], xa_send, xa_recv, (z, to))
        gsum[n_dev] = agsend[1]

    drain(some_g, ag_recv)

    @pl.when(me != last)
    def _():
        drain(gsum.at[n_dev], xa_recv)

    packed_out[...] = gsum[...]

    @pl.when(me != last)
    def _():
        drain(xsend, xr_send)

    @pl.when(me == last)
    def _():
        drain(xin.at[pl.ds(0, n_band - 1)], xz_send)
        drain(some_g, xa_send)

    drain(some, rs_send)
    drain(some_z, z_send)
    drain(some_z, t_send)
    drain(some_g, ag_send)
    for c in range(CHUNKS):
        drain(land.at[pl.ds(0, rows * (n_dev - 1)), pl.ds(c * width, width)], a2a_send.at[c])
    put_hi.wait()
    put_lo.wait()


def call_gather_gram(mesh, anomaly, ocean_mask, area_weight):
    n_band, n_dev = mesh.shape["band"], mesh.shape["dev"]
    rows, band_cells = anomaly.shape
    snaps, cells = rows * n_dev, band_cells // n_dev
    area2 = area_weight.reshape(band_cells // 128, 128)
    mask2 = ocean_mask.reshape(band_cells // 128, 128)
    f32, bf16 = jnp.float32, jnp.bfloat16
    vmem = pl.BlockSpec(memory_space=pltpu.VMEM)
    hbm = pl.BlockSpec(memory_space=pltpu.HBM)
    dma = pltpu.SemaphoreType.DMA

    def tiles(count):
        return pltpu.VMEM((count, rows, 128), f32)

    return pl.pallas_call(
        functools.partial(gather_gram, n_band, n_dev),
        name="gather_gram",
        out_shape=(jax.ShapeDtypeStruct((snaps, cells), bf16), jax.ShapeDtypeStruct((snaps, cells), bf16),
                   jax.ShapeDtypeStruct((n_dev + 1, rows, 128), f32)),
        in_specs=[hbm, hbm, hbm],
        out_specs=(hbm, hbm, vmem),
        scratch_shapes=[
            pltpu.VMEM((band_cells // 128, 128), f32), pltpu.VMEM((band_cells // 128, 128), jnp.int32),
            pltpu.VMEM((snaps, cells), f32), pltpu.VMEM((snaps, cells), bf16), pltpu.VMEM((snaps, cells), bf16),
            pltpu.VMEM((snaps, snaps), f32), tiles(n_dev + 1), tiles(n_dev), tiles(n_dev),
            pltpu.VMEM((rows, 128), f32), tiles(n_band), pltpu.VMEM((rows, 128), f32), tiles(n_band),
            pltpu.VMEM((rows, 128), f32), tiles(n_band), tiles(2), tiles(n_dev + 1),
            dma, dma, dma, dma((CHUNKS,)), dma((CHUNKS,)), *[dma] * 14, dma((2,)),
        ],
        compiler_params=pltpu.CompilerParams(collective_id=0, has_side_effects=True, vmem_limit_bytes=40 * 1024 * 1024),
        cost_estimate=pl.CostEstimate(flops=4 * snaps * snaps * cells, bytes_accessed=8 * snaps * cells, transcendentals=0),
    )(*[pltpu.with_memory_space_constraint(v, pltpu.HBM) for v in (anomaly, area2, mask2)])


PANEL = 16
TN = (((0,), (0,)), ((), ()))


def split3(x):
    a = x.astype(jnp.bfloat16)
    rest = x - a.astype(jnp.float32)
    b = rest.astype(jnp.bfloat16)
    return a, b, (rest - b.astype(jnp.float32)).astype(jnp.bfloat16)


def factor(work, upper, inverse, zero_ref, between):
    n = work.shape[0]
    zero_ref[...] = jnp.zeros((8, 128), jnp.float32)
    zero = zero_ref[...]
    row = lax.broadcasted_iota(jnp.int32, (8, 128), 0)
    lane = lax.broadcasted_iota(jnp.int32, (8, 128), 1)
    groups = PANEL // 8
    tiles = n // 128
    for k in range(n // PANEL):
        base = k * PANEL
        home, off = base // 128, base % 128
        more = base + PANEL < n
        inside = (lane >= off) & (lane < off + PANEL)
        count = 2 * groups if more else groups
        panel = [[work[base + 8 * s:base + 8 * s + 8, t * 128:(t + 1) * 128] for t in range(tiles)] for s in range(count)]
        cols = [[jnp.broadcast_to(panel[s][home][:, off + c:off + c + 1], (8, 128)) + zero for s in range(count)] for c in range(PANEL)]
        diag = [panel[s][home] for s in range(groups)]
        for s in range(count):
            unit = jnp.where(lane == row + (off + 8 * s), 1.0, 0.0) if s < groups else 0.0
            panel[s][home] = jnp.where(inside, unit, panel[s][home])
        pivots = [None] * groups
        for j in range(PANEL):
            own, r = j // 8, j % 8
            pivot = jnp.broadcast_to(cols[j][own][r:r + 1, :], (8, 128))
            pivots[own] = pivot if r == 0 else jnp.where(row >= r, pivot, pivots[own])
            inv = 1.0 / pivot
            first = own if r < 7 else own + 1
            mult = {}
            for s in range(first, count):
                m = jnp.where(row > r, cols[j][s], 0.0) if s == own else cols[j][s]
                mult[s] = m * inv
            for c in range(j + 1, PANEL):
                line = jnp.broadcast_to(cols[c][own][r:r + 1, :], (8, 128))
                for s in range(first, count):
                    if s >= groups or 8 * s + 7 > j:
                        cols[c][s] = cols[c][s] - mult[s] * line
            for t in range(tiles):
                line = jnp.broadcast_to(panel[own][t][r:r + 1, :], (8, 128))
                for s in range(first, count):
                    panel[s][t] = panel[s][t] - mult[s] * line
            line = jnp.broadcast_to(diag[own][r:r + 1, :], (8, 128))
            for s in range(first, groups):
                diag[s] = diag[s] - mult[s] * line
        for s in range(groups):
            scale = lax.rsqrt(pivots[s])
            at = pl.ds(base + 8 * s, 8)
            for t in range(tiles):
                val = panel[s][t] * scale
                panel[s][t] = val
                wide = pl.ds(t * 128, 128)
                if t < home:
                    inverse[at, wide] = val
                    upper[at, wide] = jnp.zeros((8, 128), jnp.float32)
                elif t > home:
                    inverse[at, wide] = jnp.zeros((8, 128), jnp.float32)
                    upper[at, wide] = val
                else:
                    inverse[at, wide] = jnp.where(lane <= row + (off + 8 * s), val, 0.0)
                    u = jnp.where(inside, diag[s] * scale, val)
                    upper[at, wide] = jnp.where(lane >= row + (off + 8 * s), u, 0.0)
        if more:
            for s in range(groups, count):
                for t in range(tiles):
                    work[base + 8 * s:base + 8 * s + 8, t * 128:(t + 1) * 128] = panel[s][t]
        between(k)
        far = base + 2 * PANEL
        if far < n:
            lines = jnp.concatenate([jnp.concatenate(panel[s], axis=1) for s in range(groups)], axis=0)
            a, b, c = split3(lines)
            left = jnp.concatenate([a, a, b, a, b, c], axis=0)
            right = jnp.concatenate([a, b, a, c, b, a], axis=0)
            start = far // 128 * 128
            delta = lax.dot_general(left[:, start:], right, TN, preferred_element_type=jnp.float32)
            for i in range(far, n, 8):
                for t in range(tiles):
                    at, wide = slice(i, i + 8), slice(t * 128, (t + 1) * 128)
                    old = work[at, wide]
                    if t == home:
                        old = jnp.where(inside, 0.0, old)
                    work[at, wide] = old - delta[i - start:i - start + 8, wide]


def unpack(packed, work):
    half = work.shape[0] // 2
    count = half // 8
    row = lax.broadcasted_iota(jnp.int32, (half, half), 0)
    lane = lax.broadcasted_iota(jnp.int32, (half, half), 1)
    mixed = packed[:count].reshape(half, half)
    cross = packed[count:2 * count].reshape(half, half)
    diag = jnp.concatenate([packed[2 * count]] * count, axis=0)
    turned = mixed.T
    work[:half, :half] = jnp.where(row <= lane, mixed, turned)
    work[:half, half:] = cross
    work[half:, :half] = cross.T
    work[half:, half:] = jnp.where(row > lane, mixed, jnp.where(row == lane, diag, turned))


def solve(packed, hi_in, lo_in, upper, scores, work, inverse, zero, hi, lo, out, in_sem, out_sem):
    get_hi = pltpu.make_async_copy(hi_in, hi, in_sem.at[0])
    get_lo = pltpu.make_async_copy(lo_in, lo, in_sem.at[1])
    get_hi.start()
    get_lo.start()
    unpack(packed, work)
    n = work.shape[0]
    half = n // 2
    panels = n // PANEL
    width = 512
    chunks = hi.shape[1] // width
    held = []
    puts = []

    def split2(x):
        a = x.astype(jnp.bfloat16)
        return a, (x - a.astype(jnp.float32)).astype(jnp.bfloat16)

    def put(rows, c):
        at = pl.ds(c * width, width)
        copy = pltpu.make_async_copy(out.at[rows, at], scores.at[rows, at], out_sem.at[len(puts)])
        copy.start()
        puts.append(copy)

    def between(k):
        if k == panels // 2 - 1:
            get_hi.wait()
            get_lo.wait()
            a, b = split2(inverse[:half, :half])
            held.append(jnp.concatenate([a, a, b], axis=1))
        elif k >= panels // 2:
            for c in range((k - panels // 2) * chunks * 2 // panels, (k + 1 - panels // 2) * chunks * 2 // panels):
                at = pl.ds(c * width, width)
                right = jnp.concatenate([hi[:half, at], lo[:half, at], hi[:half, at]], axis=0)
                out[:half, at] = jnp.dot(held[0], right, preferred_element_type=jnp.float32)
                put(pl.ds(0, half), c)

    factor(work, upper, inverse, zero, between)
    a, b = split2(inverse[half:, :])
    both = jnp.concatenate([a, b], axis=0)
    for c in range(chunks):
        at = pl.ds(c * width, width)
        ab = jnp.dot(both, hi[:, at], preferred_element_type=jnp.float32)
        out[half:, at] = ab[:half] + (ab[half:] + jnp.dot(a, lo[:, at], preferred_element_type=jnp.float32))
        put(pl.ds(half, half), c)
    for copy in puts:
        copy.wait()


def call_solve(packed, hi, lo):
    snaps, cells = hi.shape
    f32, bf16 = jnp.float32, jnp.bfloat16
    vmem = pl.BlockSpec(memory_space=pltpu.VMEM)
    hbm = pl.BlockSpec(memory_space=pl.ANY)
    dma = pltpu.SemaphoreType.DMA
    return pl.pallas_call(
        solve,
        name="solve",
        out_shape=(jax.ShapeDtypeStruct((snaps, snaps), f32), jax.ShapeDtypeStruct((snaps, cells), f32)),
        in_specs=[vmem, hbm, hbm],
        out_specs=(vmem, hbm),
        scratch_shapes=[pltpu.VMEM((snaps, snaps), f32), pltpu.VMEM((snaps, snaps), f32), pltpu.VMEM((8, 128), f32),
                        pltpu.VMEM((snaps, cells), bf16), pltpu.VMEM((snaps, cells), bf16),
                        pltpu.VMEM((snaps, cells), f32), dma((2,)), dma((2 * cells // 512,))],
        compiler_params=pltpu.CompilerParams(vmem_limit_bytes=40 * 1024 * 1024),
        cost_estimate=pl.CostEstimate(flops=6 * snaps * snaps * cells, bytes_accessed=8 * snaps * cells, transcendentals=0),
    )(packed, hi, lo)


def solution(mesh):
    def on_device(anomaly, ocean_mask, area_weight):
        hi, lo, packed = call_gather_gram(mesh, anomaly, ocean_mask, area_weight)
        return call_solve(packed, hi, lo)

    return jax.shard_map(
        on_device,
        mesh=mesh,
        in_specs=(P("dev", "band"), P("band"), P("band")),
        out_specs=(P(), P(None, ("band", "dev"))),
        check_vma=False,
    )
```

```python
import functools
import jax
import jax.numpy as jnp
from jax import lax
from jax.experimental import pallas as pl
from jax.experimental.pallas import tpu as pltpu
from jax.sharding import PartitionSpec as P

MESH = pl.DeviceIdType.MESH
CHUNKS = 8
SIDE = 4


def ring(d, n):
    return min(d, n - d)


AROUND = sorted(((dx, dy, dc) for dx in range(SIDE) for dy in range(SIDE) for dc in range(2) if dx or dy or dc),
                key=lambda o: -(ring(o[0], SIDE) + ring(o[1], SIDE)))


def gather_gram(n_band, n_dev, anomaly, area_hbm, mask_hbm, hi_out, lo_out, packed_out,
                area, mask, land, hi, lo, gram, part, piece_in, extra_in, tsend, tin, zsend, zin, xsend, xin, agsend,
                load_sem, area_sem, mask_sem, a2a_send, a2a_recv, rs_send, rs_recv, t_send, t_recv, z_send, z_recv,
                ag_send, ag_recv, xr_send, xr_recv, xz_send, xz_recv, xa_send, xa_recv, keep_sem, keep_extra_sem, out_sem):
    z = lax.axis_index("band")
    me = lax.axis_index("dev")
    x, y, core = me // (2 * SIDE), lax.rem(me, 2 * SIDE) // 2, lax.rem(me, 2)
    peers = [lax.rem(x + dx, SIDE) * (2 * SIDE) + lax.rem(y + dy, SIDE) * 2 + lax.rem(core + dc, 2) for dx, dy, dc in AROUND]
    levels = [lax.rem(z + dz, n_band) for dz in sorted(range(1, n_band), key=lambda d: -ring(d, n_band))]
    snaps, cells = land.shape
    rows = snaps // n_dev
    width = cells // CHUNKS

    barrier = pltpu.get_barrier_semaphore()

    for to in peers:
        pl.semaphore_signal(barrier, inc=1, device_id=(z, to), device_id_type=MESH)
    for to in levels:
        pl.semaphore_signal(barrier, inc=1, device_id=(to, me), device_id_type=MESH)
    own = pltpu.make_async_copy(anomaly.at[:, pl.ds(pl.multiple_of(me * cells, cells), cells)],
                                land.at[pl.ds(pl.multiple_of(me * rows, rows), rows), :], load_sem)
    own.start()
    get_area = pltpu.make_async_copy(area_hbm, area, area_sem)
    get_mask = pltpu.make_async_copy(mask_hbm, mask, mask_sem)
    get_area.start()
    get_mask.start()
    pl.semaphore_wait(barrier, n_dev - 1 + n_band - 1)

    def push(src, dst, send_sem, recv_sem, to):
        pltpu.make_async_remote_copy(src_ref=src, dst_ref=dst, send_sem=send_sem, recv_sem=recv_sem,
                                     device_id=to, device_id_type=MESH).start()

    def drain(ref, sem):
        pltpu.make_async_copy(ref, ref, sem).wait()

    def send_chunk(c, _):
        column = pl.multiple_of(c * width, width)
        for to in peers:
            pltpu.make_async_remote_copy(
                src_ref=anomaly.at[:, pl.ds(pl.multiple_of(to * cells + column, width), width)],
                dst_ref=land.at[pl.ds(pl.multiple_of(me * rows, rows), rows), pl.ds(column, width)],
                send_sem=a2a_send.at[c], recv_sem=a2a_recv.at[c],
                device_id=(z, to), device_id_type=MESH).start()
        return _
    lax.fori_loop(0, CHUNKS, send_chunk, 0)

    get_area.wait()
    get_mask.wait()
    band_total = jnp.sum(area[...] * mask[...].astype(jnp.float32))
    tsend[...] = jnp.full((rows, 128), band_total, jnp.float32)
    tin[z] = tsend[...]
    for to in levels:
        push(tsend, tin.at[z], t_send, t_recv, (to, me))
    mine = pl.ds(pl.multiple_of(me * (cells // 128), 8), cells // 128)
    root = jnp.sqrt(area[mine, :] * mask[mine, :].astype(jnp.float32))
    gram[...] = jnp.zeros_like(gram)
    own.wait()
    nt = (((1,), (1,)), ((), ()))
    done = []
    for c in range(CHUNKS):
        window = land.at[pl.ds(0, rows * (n_dev - 1)), pl.ds(c * width, width)]
        pltpu.make_async_copy(window, window, a2a_recv.at[c]).wait()
        for t in range(width // 128):
            k = c * (width // 128) + t
            at = pl.ds(k * 128, 128)
            x = land[:, at] * root[k:k + 1, :]
            top = x.astype(jnp.bfloat16)
            hi[:, at] = top
            lo[:, at] = (x - top.astype(jnp.float32)).astype(jnp.bfloat16)
        at = pl.ds(c * width, width)
        puts = [pltpu.make_async_copy(hi.at[:, at], hi_out.at[:, at], out_sem.at[2 * c]),
                pltpu.make_async_copy(lo.at[:, at], lo_out.at[:, at], out_sem.at[2 * c + 1])]
        for put in puts:
            put.start()
        done.extend(puts)
        a, b = hi[:, at], lo[:, at]
        gram[...] += (lax.dot_general(a, a, nt, preferred_element_type=jnp.float32)
                    + (lax.dot_general(a, b, nt, preferred_element_type=jnp.float32)
                       + lax.dot_general(b, a, nt, preferred_element_type=jnp.float32)))
    row = lax.broadcasted_iota(jnp.int32, (8, 128), 0)
    lane = lax.broadcasted_iota(jnp.int32, (8, 128), 1)
    half = snaps // 2
    tiles = half // 8
    extra = jnp.zeros((8, 128), jnp.float32)
    for p in range(tiles):
        corner = gram[half + 8 * p:half + 8 * p + 8, half:]
        part[p] = jnp.where(row + 8 * p <= lane, gram[8 * p:8 * p + 8, :half], corner)
        part[tiles + p] = gram[8 * p:8 * p + 8, half:]
        extra = jnp.where(row + 8 * p == lane, corner, extra)
    part[2 * tiles] = extra
    last = n_dev - 1

    for to in peers:
        push(part.at[to], piece_in.at[me], rs_send, rs_recv, (z, to))

    @pl.when(me != last)
    def _():
        push(part.at[n_dev], extra_in.at[me], xr_send, xr_recv, (z, last))

    piece_in[me] = part[me]
    drain(tin.at[pl.ds(0, n_band - 1)], t_recv)
    total = jnp.sum(tin[...], axis=0)
    some = piece_in.at[pl.ds(0, n_dev - 1)]
    some_z = zin.at[pl.ds(0, n_band - 1)]
    some_g = packed_out.at[pl.ds(0, n_dev - 1)]
    drain(some, rs_recv)
    zsend[...] = jnp.sum(piece_in[...], axis=0)
    for to in levels:
        push(zsend, zin.at[z], z_send, z_recv, (to, me))
    zin[z] = zsend[...]

    @pl.when(me == last)
    def _():
        extra_in[last] = part[n_dev]
        drain(extra_in.at[pl.ds(0, n_dev - 1)], xr_recv)
        xsend[...] = jnp.sum(extra_in[...], axis=0)
        for to in levels:
            push(xsend, xin.at[z], xz_send, xz_recv, (to, me))
        xin[z] = xsend[...]

    drain(some_z, z_recv)
    agsend[0] = jnp.sum(zin[...], axis=0) / total
    for to in peers:
        push(agsend.at[0], packed_out.at[me], ag_send, ag_recv, (z, to))
    keep = pltpu.make_async_copy(agsend.at[0], packed_out.at[me], keep_sem)
    keep.start()

    @pl.when(me == last)
    def _():
        drain(xin.at[pl.ds(0, n_band - 1)], xz_recv)
        agsend[1] = jnp.sum(xin[...], axis=0) / total
        for to in peers:
            push(agsend.at[1], packed_out.at[n_dev], xa_send, xa_recv, (z, to))
        keep_extra = pltpu.make_async_copy(agsend.at[1], packed_out.at[n_dev], keep_extra_sem)
        keep_extra.start()
        keep_extra.wait()

    drain(some_g, ag_recv)

    @pl.when(me != last)
    def _():
        drain(packed_out.at[n_dev], xa_recv)

    keep.wait()

    @pl.when(me != last)
    def _():
        drain(xsend, xr_send)

    @pl.when(me == last)
    def _():
        drain(xin.at[pl.ds(0, n_band - 1)], xz_send)
        drain(some_g, xa_send)

    drain(some, rs_send)
    drain(some_z, z_send)
    drain(some_z, t_send)
    drain(some_g, ag_send)
    for c in range(CHUNKS):
        drain(land.at[pl.ds(0, rows * (n_dev - 1)), pl.ds(c * width, width)], a2a_send.at[c])
    for put in done:
        put.wait()


def call_gather_gram(mesh, anomaly, ocean_mask, area_weight):
    n_band, n_dev = mesh.shape["band"], mesh.shape["dev"]
    rows, band_cells = anomaly.shape
    snaps, cells = rows * n_dev, band_cells // n_dev
    area2 = area_weight.reshape(band_cells // 128, 128)
    mask2 = ocean_mask.reshape(band_cells // 128, 128)
    f32, bf16 = jnp.float32, jnp.bfloat16
    vmem = pl.BlockSpec(memory_space=pltpu.VMEM)
    hbm = pl.BlockSpec(memory_space=pltpu.HBM)
    dma = pltpu.SemaphoreType.DMA

    def tiles(count):
        return pltpu.VMEM((count, rows, 128), f32)

    return pl.pallas_call(
        functools.partial(gather_gram, n_band, n_dev),
        name="gather_gram",
        out_shape=(jax.ShapeDtypeStruct((snaps, cells), bf16), jax.ShapeDtypeStruct((snaps, cells), bf16),
                   jax.ShapeDtypeStruct((n_dev + 1, rows, 128), f32)),
        in_specs=[hbm, hbm, hbm],
        out_specs=(hbm, hbm, hbm),
        scratch_shapes=[
            pltpu.VMEM((band_cells // 128, 128), f32), pltpu.VMEM((band_cells // 128, 128), jnp.int32),
            pltpu.VMEM((snaps, cells), f32), pltpu.VMEM((snaps, cells), bf16), pltpu.VMEM((snaps, cells), bf16),
            pltpu.VMEM((snaps, snaps), f32), tiles(n_dev + 1), tiles(n_dev), tiles(n_dev),
            pltpu.VMEM((rows, 128), f32), tiles(n_band), pltpu.VMEM((rows, 128), f32), tiles(n_band),
            pltpu.VMEM((rows, 128), f32), tiles(n_band), tiles(2),
            dma, dma, dma, dma((CHUNKS,)), dma((CHUNKS,)), *[dma] * 16, dma((2 * CHUNKS,)),
        ],
        compiler_params=pltpu.CompilerParams(collective_id=0, has_side_effects=True, vmem_limit_bytes=40 * 1024 * 1024),
        cost_estimate=pl.CostEstimate(flops=4 * snaps * snaps * cells, bytes_accessed=8 * snaps * cells, transcendentals=0),
    )(*[pltpu.with_memory_space_constraint(v, pltpu.HBM) for v in (anomaly, area2, mask2)])


PANEL = 16
TN = (((0,), (0,)), ((), ()))


def split3(x):
    a = x.astype(jnp.bfloat16)
    rest = x - a.astype(jnp.float32)
    b = rest.astype(jnp.bfloat16)
    return a, b, (rest - b.astype(jnp.float32)).astype(jnp.bfloat16)


def factor(work, upper, inverse, zero_ref, between):
    n = work.shape[0]
    zero_ref[...] = jnp.zeros((8, 128), jnp.float32)
    zero = zero_ref[...]
    row = lax.broadcasted_iota(jnp.int32, (8, 128), 0)
    lane = lax.broadcasted_iota(jnp.int32, (8, 128), 1)
    groups = PANEL // 8
    tiles = n // 128
    for k in range(n // PANEL):
        base = k * PANEL
        home, off = base // 128, base % 128
        more = base + PANEL < n
        inside = (lane >= off) & (lane < off + PANEL)
        count = 2 * groups if more else groups
        panel = [[work[base + 8 * s:base + 8 * s + 8, t * 128:(t + 1) * 128] for t in range(tiles)] for s in range(count)]
        cols = [[jnp.broadcast_to(panel[s][home][:, off + c:off + c + 1], (8, 128)) for s in range(count)] for c in range(PANEL)]
        cols[0] = [v + zero for v in cols[0][:groups]] + cols[0][groups:]
        diag = [panel[s][home] for s in range(groups)]
        for s in range(count):
            unit = jnp.where(lane == row + (off + 8 * s), 1.0, 0.0) if s < groups else 0.0
            panel[s][home] = jnp.where(inside, unit, panel[s][home])
        pivots = [None] * groups
        for j in range(PANEL):
            own, r = j // 8, j % 8
            pivot = jnp.broadcast_to(cols[j][own][r:r + 1, :], (8, 128))
            pivots[own] = pivot if r == 0 else jnp.where(row >= r, pivot, pivots[own])
            inv = 1.0 / pivot
            first = own if r < 7 else own + 1
            mult = {}
            for s in range(first, count):
                m = jnp.where(row > r, cols[j][s], 0.0) if s == own else cols[j][s]
                mult[s] = m * inv
            for c in range(j + 1, PANEL):
                line = jnp.broadcast_to(cols[j][c // 8][c % 8:c % 8 + 1, :], (8, 128))
                for s in range(max(first, c // 8), count):
                    cols[c][s] = cols[c][s] - mult[s] * line
            for t in range(tiles):
                line = jnp.broadcast_to(panel[own][t][r:r + 1, :], (8, 128))
                for s in range(first, count):
                    panel[s][t] = panel[s][t] - mult[s] * line
            line = jnp.broadcast_to(diag[own][r:r + 1, :], (8, 128))
            for s in range(first, groups):
                diag[s] = diag[s] - mult[s] * line
        for s in range(groups):
            scale = lax.rsqrt(pivots[s])
            at = pl.ds(base + 8 * s, 8)
            for t in range(tiles):
                val = panel[s][t] * scale
                panel[s][t] = val
                wide = pl.ds(t * 128, 128)
                if t < home:
                    inverse[at, wide] = val
                    upper[at, wide] = jnp.zeros((8, 128), jnp.float32)
                elif t > home:
                    inverse[at, wide] = jnp.zeros((8, 128), jnp.float32)
                    upper[at, wide] = val
                else:
                    inverse[at, wide] = jnp.where(lane <= row + (off + 8 * s), val, 0.0)
                    u = jnp.where(inside, diag[s] * scale, val)
                    upper[at, wide] = jnp.where(lane >= row + (off + 8 * s), u, 0.0)
        if more:
            for s in range(groups, count):
                for t in range(tiles):
                    work[base + 8 * s:base + 8 * s + 8, t * 128:(t + 1) * 128] = panel[s][t]
        between(k)
        far = base + 2 * PANEL
        if far < n:
            lines = jnp.concatenate([jnp.concatenate(panel[s], axis=1) for s in range(groups)], axis=0)
            a, b, c = split3(lines)
            left = jnp.concatenate([a, a, b, a, b, c], axis=0)
            right = jnp.concatenate([a, b, a, c, b, a], axis=0)
            start = far // 128 * 128
            delta = lax.dot_general(left[:, start:], right, TN, preferred_element_type=jnp.float32)
            for i in range(far, n, 8):
                for t in range(tiles):
                    at, wide = slice(i, i + 8), slice(t * 128, (t + 1) * 128)
                    old = work[at, wide]
                    if t == home:
                        old = jnp.where(inside, 0.0, old)
                    work[at, wide] = old - delta[i - start:i - start + 8, wide]


def unpack(packed, work):
    half = work.shape[0] // 2
    count = half // 8
    row = lax.broadcasted_iota(jnp.int32, (half, half), 0)
    lane = lax.broadcasted_iota(jnp.int32, (half, half), 1)
    mixed = packed[:count].reshape(half, half)
    cross = packed[count:2 * count].reshape(half, half)
    diag = jnp.concatenate([packed[2 * count]] * count, axis=0)
    turned = mixed.T
    work[:half, :half] = jnp.where(row <= lane, mixed, turned)
    work[:half, half:] = cross
    work[half:, :half] = cross.T
    work[half:, half:] = jnp.where(row > lane, mixed, jnp.where(row == lane, diag, turned))


def solve(packed, hi_in, lo_in, factor_out, scores, work, upper, inverse, zero, hi, lo, out, in_sem, factor_sem, out_sem):
    get_hi = pltpu.make_async_copy(hi_in, hi, in_sem.at[0])
    get_lo = pltpu.make_async_copy(lo_in, lo, in_sem.at[1])
    get_hi.start()
    get_lo.start()
    unpack(packed, work)
    n = work.shape[0]
    half = n // 2
    panels = n // PANEL
    width = 512
    chunks = hi.shape[1] // width
    held = []
    puts = []

    def split2(x):
        a = x.astype(jnp.bfloat16)
        return a, (x - a.astype(jnp.float32)).astype(jnp.bfloat16)

    def put(rows, c):
        at = pl.ds(c * width, width)
        copy = pltpu.make_async_copy(out.at[rows, at], scores.at[rows, at], out_sem.at[len(puts)])
        copy.start()
        puts.append(copy)

    def between(k):
        if k == panels // 2 - 1:
            get_hi.wait()
            get_lo.wait()
            a, b = split2(inverse[:half, :half])
            held.append(jnp.concatenate([a, a, b], axis=1))
        elif k >= panels // 2:
            for c in range((k - panels // 2) * chunks * 2 // panels, (k + 1 - panels // 2) * chunks * 2 // panels):
                at = pl.ds(c * width, width)
                right = jnp.concatenate([hi[:half, at], lo[:half, at], hi[:half, at]], axis=0)
                out[:half, at] = jnp.dot(held[0], right, preferred_element_type=jnp.float32)
                put(pl.ds(0, half), c)

    factor(work, upper, inverse, zero, between)
    put_factor = pltpu.make_async_copy(upper, factor_out, factor_sem)
    put_factor.start()
    a, b = split2(inverse[half:, :])
    both = jnp.concatenate([a, b], axis=0)
    for c in range(chunks):
        at = pl.ds(c * width, width)
        ab = jnp.dot(both, hi[:, at], preferred_element_type=jnp.float32)
        out[half:, at] = ab[:half] + (ab[half:] + jnp.dot(a, lo[:, at], preferred_element_type=jnp.float32))
        put(pl.ds(half, half), c)
    for copy in puts:
        copy.wait()
    put_factor.wait()


def call_solve(packed, hi, lo):
    snaps, cells = hi.shape
    f32, bf16 = jnp.float32, jnp.bfloat16
    vmem = pl.BlockSpec(memory_space=pltpu.VMEM)
    hbm = pl.BlockSpec(memory_space=pl.ANY)
    dma = pltpu.SemaphoreType.DMA
    return pl.pallas_call(
        solve,
        name="solve",
        out_shape=(jax.ShapeDtypeStruct((snaps, snaps), f32), jax.ShapeDtypeStruct((snaps, cells), f32)),
        in_specs=[vmem, hbm, hbm],
        out_specs=(hbm, hbm),
        scratch_shapes=[pltpu.VMEM((snaps, snaps), f32), pltpu.VMEM((snaps, snaps), f32), pltpu.VMEM((snaps, snaps), f32),
                        pltpu.VMEM((8, 128), f32),
                        pltpu.VMEM((snaps, cells), bf16), pltpu.VMEM((snaps, cells), bf16),
                        pltpu.VMEM((snaps, cells), f32), dma((2,)), dma, dma((2 * cells // 512,))],
        compiler_params=pltpu.CompilerParams(vmem_limit_bytes=40 * 1024 * 1024),
        cost_estimate=pl.CostEstimate(flops=6 * snaps * snaps * cells, bytes_accessed=8 * snaps * cells, transcendentals=0),
    )(packed, hi, lo)


def solution(mesh):
    def on_device(anomaly, ocean_mask, area_weight):
        hi, lo, packed = call_gather_gram(mesh, anomaly, ocean_mask, area_weight)
        return call_solve(packed, hi, lo)

    return jax.shard_map(
        on_device,
        mesh=mesh,
        in_specs=(P("dev", "band"), P("band"), P("band")),
        out_specs=(P(), P(None, ("band", "dev"))),
        check_vma=False,
    )
```

```python
import functools
import jax
import jax.numpy as jnp
from jax import lax
from jax.experimental import pallas as pl
from jax.experimental.pallas import tpu as pltpu
from jax.sharding import PartitionSpec as P

MESH = pl.DeviceIdType.MESH
CHUNKS = 8
SIDE = 4


def ring(d, n):
    return min(d, n - d)


AROUND = sorted(((dx, dy, dc) for dx in range(SIDE) for dy in range(SIDE) for dc in range(2) if dx or dy or dc),
                key=lambda o: -(ring(o[0], SIDE) + ring(o[1], SIDE)))


def gather_gram(n_band, n_dev, anomaly, area_hbm, mask_hbm, hi, lo, packed_out,
                area, mask, land, gram, part, piece_in, extra_in, tsend, tin, zsend, zin, xsend, xin, agsend,
                load_sem, area_sem, mask_sem, a2a_send, a2a_recv, rs_send, rs_recv, t_send, t_recv, z_send, z_recv,
                ag_send, ag_recv, xr_send, xr_recv, xz_send, xz_recv, xa_send, xa_recv, keep_sem, keep_extra_sem):
    z = lax.axis_index("band")
    me = lax.axis_index("dev")
    x, y, core = me // (2 * SIDE), lax.rem(me, 2 * SIDE) // 2, lax.rem(me, 2)
    peers = [lax.rem(x + dx, SIDE) * (2 * SIDE) + lax.rem(y + dy, SIDE) * 2 + lax.rem(core + dc, 2) for dx, dy, dc in AROUND]
    levels = [lax.rem(z + dz, n_band) for dz in sorted(range(1, n_band), key=lambda d: -ring(d, n_band))]
    snaps, cells = land.shape
    rows = snaps // n_dev
    width = cells // CHUNKS

    barrier = pltpu.get_barrier_semaphore()

    for to in peers:
        pl.semaphore_signal(barrier, inc=1, device_id=(z, to), device_id_type=MESH)
    for to in levels:
        pl.semaphore_signal(barrier, inc=1, device_id=(to, me), device_id_type=MESH)
    own = pltpu.make_async_copy(anomaly.at[:, pl.ds(pl.multiple_of(me * cells, cells), cells)],
                                land.at[pl.ds(pl.multiple_of(me * rows, rows), rows), :], load_sem)
    own.start()
    get_area = pltpu.make_async_copy(area_hbm, area, area_sem)
    get_mask = pltpu.make_async_copy(mask_hbm, mask, mask_sem)
    get_area.start()
    get_mask.start()
    pl.semaphore_wait(barrier, n_dev - 1 + n_band - 1)

    def push(src, dst, send_sem, recv_sem, to):
        pltpu.make_async_remote_copy(src_ref=src, dst_ref=dst, send_sem=send_sem, recv_sem=recv_sem,
                                     device_id=to, device_id_type=MESH).start()

    def drain(ref, sem):
        pltpu.make_async_copy(ref, ref, sem).wait()

    def send_chunk(c, _):
        column = pl.multiple_of(c * width, width)
        for to in peers:
            pltpu.make_async_remote_copy(
                src_ref=anomaly.at[:, pl.ds(pl.multiple_of(to * cells + column, width), width)],
                dst_ref=land.at[pl.ds(pl.multiple_of(me * rows, rows), rows), pl.ds(column, width)],
                send_sem=a2a_send.at[c], recv_sem=a2a_recv.at[c],
                device_id=(z, to), device_id_type=MESH).start()
        return _
    lax.fori_loop(0, CHUNKS, send_chunk, 0)

    get_area.wait()
    get_mask.wait()
    band_total = jnp.sum(area[...] * mask[...].astype(jnp.float32))
    tsend[...] = jnp.full((rows, 128), band_total, jnp.float32)
    tin[z] = tsend[...]
    for to in levels:
        push(tsend, tin.at[z], t_send, t_recv, (to, me))
    mine = pl.ds(pl.multiple_of(me * (cells // 128), 8), cells // 128)
    root = jnp.sqrt(area[mine, :] * mask[mine, :].astype(jnp.float32))
    gram[...] = jnp.zeros_like(gram)
    own.wait()
    nt = (((1,), (1,)), ((), ()))
    for c in range(CHUNKS):
        window = land.at[pl.ds(0, rows * (n_dev - 1)), pl.ds(c * width, width)]
        pltpu.make_async_copy(window, window, a2a_recv.at[c]).wait()
        for t in range(width // 128):
            k = c * (width // 128) + t
            at = pl.ds(k * 128, 128)
            x = land[:, at] * root[k:k + 1, :]
            top = x.astype(jnp.bfloat16)
            hi[:, at] = top
            lo[:, at] = (x - top.astype(jnp.float32)).astype(jnp.bfloat16)
        at = pl.ds(c * width, width)
        a, b = hi[:, at], lo[:, at]
        gram[...] += (lax.dot_general(a, a, nt, preferred_element_type=jnp.float32)
                    + (lax.dot_general(a, b, nt, preferred_element_type=jnp.float32)
                       + lax.dot_general(b, a, nt, preferred_element_type=jnp.float32)))
    row = lax.broadcasted_iota(jnp.int32, (8, 128), 0)
    lane = lax.broadcasted_iota(jnp.int32, (8, 128), 1)
    half = snaps // 2
    tiles = half // 8
    extra = jnp.zeros((8, 128), jnp.float32)
    for p in range(tiles):
        corner = gram[half + 8 * p:half + 8 * p + 8, half:]
        part[p] = jnp.where(row + 8 * p <= lane, gram[8 * p:8 * p + 8, :half], corner)
        part[tiles + p] = gram[8 * p:8 * p + 8, half:]
        extra = jnp.where(row + 8 * p == lane, corner, extra)
    part[2 * tiles] = extra
    last = n_dev - 1

    for to in peers:
        push(part.at[to], piece_in.at[me], rs_send, rs_recv, (z, to))

    @pl.when(me != last)
    def _():
        push(part.at[n_dev], extra_in.at[me], xr_send, xr_recv, (z, last))

    piece_in[me] = part[me]
    drain(tin.at[pl.ds(0, n_band - 1)], t_recv)
    total = jnp.sum(tin[...], axis=0)
    some = piece_in.at[pl.ds(0, n_dev - 1)]
    some_z = zin.at[pl.ds(0, n_band - 1)]
    some_g = packed_out.at[pl.ds(0, n_dev - 1)]
    drain(some, rs_recv)
    zsend[...] = jnp.sum(piece_in[...], axis=0)
    for to in levels:
        push(zsend, zin.at[z], z_send, z_recv, (to, me))
    zin[z] = zsend[...]

    @pl.when(me == last)
    def _():
        extra_in[last] = part[n_dev]
        drain(extra_in.at[pl.ds(0, n_dev - 1)], xr_recv)
        xsend[...] = jnp.sum(extra_in[...], axis=0)
        for to in levels:
            push(xsend, xin.at[z], xz_send, xz_recv, (to, me))
        xin[z] = xsend[...]

    drain(some_z, z_recv)
    agsend[0] = jnp.sum(zin[...], axis=0) / total
    for to in peers:
        push(agsend.at[0], packed_out.at[me], ag_send, ag_recv, (z, to))
    keep = pltpu.make_async_copy(agsend.at[0], packed_out.at[me], keep_sem)
    keep.start()

    @pl.when(me == last)
    def _():
        drain(xin.at[pl.ds(0, n_band - 1)], xz_recv)
        agsend[1] = jnp.sum(xin[...], axis=0) / total
        for to in peers:
            push(agsend.at[1], packed_out.at[n_dev], xa_send, xa_recv, (z, to))
        keep_extra = pltpu.make_async_copy(agsend.at[1], packed_out.at[n_dev], keep_extra_sem)
        keep_extra.start()
        keep_extra.wait()

    drain(some_g, ag_recv)

    @pl.when(me != last)
    def _():
        drain(packed_out.at[n_dev], xa_recv)

    keep.wait()

    @pl.when(me != last)
    def _():
        drain(xsend, xr_send)

    @pl.when(me == last)
    def _():
        drain(xin.at[pl.ds(0, n_band - 1)], xz_send)
        drain(some_g, xa_send)

    drain(some, rs_send)
    drain(some_z, z_send)
    drain(some_z, t_send)
    drain(some_g, ag_send)
    for c in range(CHUNKS):
        drain(land.at[pl.ds(0, rows * (n_dev - 1)), pl.ds(c * width, width)], a2a_send.at[c])


def call_gather_gram(mesh, anomaly, ocean_mask, area_weight):
    n_band, n_dev = mesh.shape["band"], mesh.shape["dev"]
    rows, band_cells = anomaly.shape
    snaps, cells = rows * n_dev, band_cells // n_dev
    area2 = area_weight.reshape(band_cells // 128, 128)
    mask2 = ocean_mask.reshape(band_cells // 128, 128)
    f32, bf16 = jnp.float32, jnp.bfloat16
    vmem = pl.BlockSpec(memory_space=pltpu.VMEM)
    hbm = pl.BlockSpec(memory_space=pltpu.HBM)
    dma = pltpu.SemaphoreType.DMA

    def tiles(count):
        return pltpu.VMEM((count, rows, 128), f32)

    return pl.pallas_call(
        functools.partial(gather_gram, n_band, n_dev),
        name="gather_gram",
        out_shape=(jax.ShapeDtypeStruct((snaps, cells), bf16), jax.ShapeDtypeStruct((snaps, cells), bf16),
                   jax.ShapeDtypeStruct((n_dev + 1, rows, 128), f32)),
        in_specs=[hbm, hbm, hbm],
        out_specs=(vmem, vmem, hbm),
        scratch_shapes=[
            pltpu.VMEM((band_cells // 128, 128), f32), pltpu.VMEM((band_cells // 128, 128), jnp.int32),
            pltpu.VMEM((snaps, cells), f32),
            pltpu.VMEM((snaps, snaps), f32), tiles(n_dev + 1), tiles(n_dev), tiles(n_dev),
            pltpu.VMEM((rows, 128), f32), tiles(n_band), pltpu.VMEM((rows, 128), f32), tiles(n_band),
            pltpu.VMEM((rows, 128), f32), tiles(n_band), tiles(2),
            dma, dma, dma, dma((CHUNKS,)), dma((CHUNKS,)), *[dma] * 16,
        ],
        compiler_params=pltpu.CompilerParams(collective_id=0, has_side_effects=True, vmem_limit_bytes=40 * 1024 * 1024),
        cost_estimate=pl.CostEstimate(flops=4 * snaps * snaps * cells, bytes_accessed=8 * snaps * cells, transcendentals=0),
    )(*[pltpu.with_memory_space_constraint(v, pltpu.HBM) for v in (anomaly, area2, mask2)])


PANEL = 16
TN = (((0,), (0,)), ((), ()))


def split3(x):
    a = x.astype(jnp.bfloat16)
    rest = x - a.astype(jnp.float32)
    b = rest.astype(jnp.bfloat16)
    return a, b, (rest - b.astype(jnp.float32)).astype(jnp.bfloat16)


def factor(work, upper, inverse, zero_ref, between):
    n = work.shape[0]
    zero_ref[...] = jnp.zeros((8, 128), jnp.float32)
    zero = zero_ref[...]
    row = lax.broadcasted_iota(jnp.int32, (8, 128), 0)
    lane = lax.broadcasted_iota(jnp.int32, (8, 128), 1)
    groups = PANEL // 8
    tiles = n // 128
    for k in range(n // PANEL):
        base = k * PANEL
        home, off = base // 128, base % 128
        more = base + PANEL < n
        inside = (lane >= off) & (lane < off + PANEL)
        count = 2 * groups if more else groups
        panel = [[work[base + 8 * s:base + 8 * s + 8, t * 128:(t + 1) * 128] for t in range(tiles)] for s in range(count)]
        cols = [[jnp.broadcast_to(panel[s][home][:, off + c:off + c + 1], (8, 128)) for s in range(count)] for c in range(PANEL)]
        cols[0] = [v + zero for v in cols[0][:groups]] + cols[0][groups:]
        diag = [panel[s][home] for s in range(groups)]
        for s in range(count):
            unit = jnp.where(lane == row + (off + 8 * s), 1.0, 0.0) if s < groups else 0.0
            panel[s][home] = jnp.where(inside, unit, panel[s][home])
        pivots = [None] * groups
        for j in range(PANEL):
            own, r = j // 8, j % 8
            pivot = jnp.broadcast_to(cols[j][own][r:r + 1, :], (8, 128))
            pivots[own] = pivot if r == 0 else jnp.where(row >= r, pivot, pivots[own])
            inv = 1.0 / pivot
            first = own if r < 7 else own + 1
            mult = {}
            for s in range(first, count):
                m = jnp.where(row > r, cols[j][s], 0.0) if s == own else cols[j][s]
                mult[s] = m * inv
            for c in range(j + 1, PANEL):
                line = jnp.broadcast_to(cols[j][c // 8][c % 8:c % 8 + 1, :], (8, 128))
                for s in range(max(first, c // 8), count):
                    cols[c][s] = cols[c][s] - mult[s] * line
            for t in range(tiles):
                line = jnp.broadcast_to(panel[own][t][r:r + 1, :], (8, 128))
                for s in range(first, count):
                    panel[s][t] = panel[s][t] - mult[s] * line
            line = jnp.broadcast_to(diag[own][r:r + 1, :], (8, 128))
            for s in range(first, groups):
                diag[s] = diag[s] - mult[s] * line
        for s in range(groups):
            scale = lax.rsqrt(pivots[s])
            at = pl.ds(base + 8 * s, 8)
            for t in range(tiles):
                val = panel[s][t] * scale
                panel[s][t] = val
                wide = pl.ds(t * 128, 128)
                if t < home:
                    inverse[at, wide] = val
                    upper[at, wide] = jnp.zeros((8, 128), jnp.float32)
                elif t > home:
                    inverse[at, wide] = jnp.zeros((8, 128), jnp.float32)
                    upper[at, wide] = val
                else:
                    inverse[at, wide] = jnp.where(lane <= row + (off + 8 * s), val, 0.0)
                    u = jnp.where(inside, diag[s] * scale, val)
                    upper[at, wide] = jnp.where(lane >= row + (off + 8 * s), u, 0.0)
        if more:
            for s in range(groups, count):
                for t in range(tiles):
                    work[base + 8 * s:base + 8 * s + 8, t * 128:(t + 1) * 128] = panel[s][t]
        between(k)
        far = base + 2 * PANEL
        if far < n:
            lines = jnp.concatenate([jnp.concatenate(panel[s], axis=1) for s in range(groups)], axis=0)
            a, b, c = split3(lines)
            left = jnp.concatenate([a, a, b, a, b, c], axis=0)
            right = jnp.concatenate([a, b, a, c, b, a], axis=0)
            start = far // 128 * 128
            delta = lax.dot_general(left[:, start:], right, TN, preferred_element_type=jnp.float32)
            for i in range(far, n, 8):
                for t in range(tiles):
                    at, wide = slice(i, i + 8), slice(t * 128, (t + 1) * 128)
                    old = work[at, wide]
                    if t == home:
                        old = jnp.where(inside, 0.0, old)
                    work[at, wide] = old - delta[i - start:i - start + 8, wide]


def unpack(packed, work):
    half = work.shape[0] // 2
    count = half // 8
    row = lax.broadcasted_iota(jnp.int32, (half, half), 0)
    lane = lax.broadcasted_iota(jnp.int32, (half, half), 1)
    mixed = packed[:count].reshape(half, half)
    cross = packed[count:2 * count].reshape(half, half)
    diag = jnp.concatenate([packed[2 * count]] * count, axis=0)
    turned = mixed.T
    work[:half, :half] = jnp.where(row <= lane, mixed, turned)
    work[:half, half:] = cross
    work[half:, :half] = cross.T
    work[half:, half:] = jnp.where(row > lane, mixed, jnp.where(row == lane, diag, turned))


def solve(packed, hi, lo, factor_out, scores, work, upper, inverse, zero, out, factor_sem, out_sem):
    unpack(packed, work)
    n = work.shape[0]
    half = n // 2
    panels = n // PANEL
    width = 512
    chunks = hi.shape[1] // width
    held = []
    puts = []

    def split2(x):
        a = x.astype(jnp.bfloat16)
        return a, (x - a.astype(jnp.float32)).astype(jnp.bfloat16)

    def put(rows, c):
        at = pl.ds(c * width, width)
        copy = pltpu.make_async_copy(out.at[rows, at], scores.at[rows, at], out_sem.at[len(puts)])
        copy.start()
        puts.append(copy)

    def between(k):
        if k == panels // 2 - 1:
            a, b = split2(inverse[:half, :half])
            held.append(jnp.concatenate([a, a, b], axis=1))
        elif k >= panels // 2:
            for c in range((k - panels // 2) * chunks * 2 // panels, (k + 1 - panels // 2) * chunks * 2 // panels):
                at = pl.ds(c * width, width)
                right = jnp.concatenate([hi[:half, at], lo[:half, at], hi[:half, at]], axis=0)
                out[:half, at] = jnp.dot(held[0], right, preferred_element_type=jnp.float32)
                put(pl.ds(0, half), c)

    factor(work, upper, inverse, zero, between)
    put_factor = pltpu.make_async_copy(upper, factor_out, factor_sem)
    put_factor.start()
    a, b = split2(inverse[half:, :])
    both = jnp.concatenate([a, b], axis=0)
    for c in range(chunks):
        at = pl.ds(c * width, width)
        ab = jnp.dot(both, hi[:, at], preferred_element_type=jnp.float32)
        out[half:, at] = ab[:half] + (ab[half:] + jnp.dot(a, lo[:, at], preferred_element_type=jnp.float32))
        put(pl.ds(half, half), c)
    for copy in puts:
        copy.wait()
    put_factor.wait()


def call_solve(packed, hi, lo):
    snaps, cells = hi.shape
    f32, bf16 = jnp.float32, jnp.bfloat16
    vmem = pl.BlockSpec(memory_space=pltpu.VMEM)
    hbm = pl.BlockSpec(memory_space=pl.ANY)
    dma = pltpu.SemaphoreType.DMA
    return pl.pallas_call(
        solve,
        name="solve",
        out_shape=(jax.ShapeDtypeStruct((snaps, snaps), f32), jax.ShapeDtypeStruct((snaps, cells), f32)),
        in_specs=[vmem, vmem, vmem],
        out_specs=(hbm, hbm),
        scratch_shapes=[pltpu.VMEM((snaps, snaps), f32), pltpu.VMEM((snaps, snaps), f32), pltpu.VMEM((snaps, snaps), f32),
                        pltpu.VMEM((8, 128), f32),
                        pltpu.VMEM((snaps, cells), f32), dma, dma((2 * cells // 512,))],
        compiler_params=pltpu.CompilerParams(vmem_limit_bytes=40 * 1024 * 1024),
        cost_estimate=pl.CostEstimate(flops=6 * snaps * snaps * cells, bytes_accessed=8 * snaps * cells, transcendentals=0),
    )(packed, hi, lo)


def solution(mesh):
    def on_device(anomaly, ocean_mask, area_weight):
        hi, lo, packed = call_gather_gram(mesh, anomaly, ocean_mask, area_weight)
        return call_solve(packed, hi, lo)

    return jax.shard_map(
        on_device,
        mesh=mesh,
        in_specs=(P("dev", "band"), P("band"), P("band")),
        out_specs=(P(), P(None, ("band", "dev"))),
        check_vma=False,
    )
```
